512 devices in a mesh: mp: 4 (over z_hi), space: 128 (over y, z_lo, x, core).
Axes of the slice: x: 4, y: 4, z: 16 (z_hi: 4, z_lo: 4; z = z_hi * 4 + z_lo), core: 2. Of those that a mesh axis runs over, the one named last changes fastest.
Arguments:
- positions: float32 [3, 8192], P(None, 'space'), may hold values from 0 to 1
- send_lists: int32 [128, 6, 128], P('space'), may hold values from -1 to 575, as said below
- neighbours: int32 [96, 8192], P(None, 'space'), may hold values from -1 to 831, as said below
- emb_scale: float32 [4, 25], P('mp'), may hold values from -4 to 4
- emb_shift: float32 [4, 25], P('mp'), may hold values from -4 to 4
- emb_middle: bfloat16 [4, 50, 25], P('mp'), may hold values from -1.25 to 1.25
- emb_mid_bias: float32 [4, 50], P('mp'), may hold values from -3 to 3
- emb_outer: bfloat16 [4, 100, 50], P('mp'), may hold values from -0.875 to 0.875
- emb_out_bias: float32 [4, 100], P('mp'), may hold values from -3 to 3
- fit_first: bfloat16 [4, 240, 1600], P('mp'), may hold values from -0.078125 to 0.078125
- fit_first_bias: float32 [4, 240], P('mp'), may hold values from -3 to 3
- fit_second: bfloat16 [4, 240, 240], P('mp'), may hold values from -0.375 to 0.375
- fit_second_bias: float32 [4, 240], P('mp'), may hold values from -3 to 3
- fit_third: bfloat16 [4, 240, 240], P('mp'), may hold values from -0.375 to 0.375
- fit_third_bias: float32 [4, 240], P('mp'), may hold values from -3 to 3
- fit_readout: bfloat16 [4, 240], P('mp'), may hold values from -0.375 to 0.375
Outputs:
- mean_force: float32 [3, 128, 4, 16], P(None, 'space', 'mp')
- force_spread: float32 [128, 4, 16], P('space', 'mp')
- virial_spread: float32 [128, 4, 16], P('space', 'mp')
The draws below stay inside these ranges and needn't reach their ends.
Inputs may be any that keep to these rules, and one draw needn't show every extreme that they name: `send_lists`: direction b runs +x, -x, +y, -y, +z, -z. A list of section b // 2 names owned atoms (below 64) or live ghost slots of earlier sections of the sender's extended array; live entries come first and -1 fills the rest; each list holds 42 to 128 live entries, entries may repeat, and in every draw some domain's list in each direction is full. `neighbours`: each entry names another owned atom of the same domain or a live ghost slot of that domain's extended array; -1 marks an empty slot.
All inputs are finite; a program needn't handle non-finite values.
Results may differ from the reference program's by a relative error of at most 0.012.
Values sent between devices are 32-bit elements; how exact they have to be, the bound alone decides.
No kernel may reach another device: no remote copies, remote signals or barrier semaphores. Data moves between devices by JAX's collectives and lax.ppermute only.
A program may use at most 64 MiB of HBM per device.

```python
import jax
import jax.numpy as jnp
from jax import lax

E1 = 25
E2 = 50
E3 = 100
AXIS = 16
FIT = 240
K = 96
A_DEV = 64
CAP = 128
MODELS = 4
DOMAINS = 128
GY = 4
GZ = 4
ATOMS = 8192
QUART = 16


def live_counts(key):
    base = jax.random.fold_in(key, 7001)
    counts = jax.random.randint(jax.random.fold_in(base, 1), (DOMAINS, 6), CAP // 3, CAP + 1)
    chosen_full = jax.random.randint(jax.random.fold_in(base, 2), (6,), 0, DOMAINS)
    row_ids = jnp.arange(DOMAINS)[:, None]
    return jnp.where(row_ids == chosen_full[None, :], CAP, counts).astype(jnp.int32)


def received_counts(counts):
    strides = (GY * GZ, GZ, 1)
    columns = []
    for block_id in range(6):
        section_id = block_id // 2
        step_by = strides[section_id] if block_id % 2 == 0 else -strides[section_id]
        columns.append(jnp.roll(counts[:, block_id], step_by, axis=0))
    return jnp.stack(columns, axis=1)


def slot_of(picked, counts, block_count):
    result = picked
    first_col = jnp.full_like(picked, A_DEV)
    for block_id in range(block_count):
        length = counts[..., block_id]
        inside = (picked >= first_col) & (picked < first_col + length)
        result = jnp.where(inside, A_DEV + block_id * CAP + (picked - first_col), result)
        first_col = first_col + length
    return result


def draw_send_lists(key, part):
    counts = live_counts(key)
    arrived = received_counts(counts)
    results = []
    for block_id in range(6):
        section_id = block_id // 2
        upper = A_DEV + jnp.sum(arrived[:, :2 * section_id], axis=1, keepdims=True)
        picked = jax.random.randint(jax.random.fold_in(key, 7100 + block_id), (DOMAINS, CAP), 0, upper)
        slots = slot_of(picked, arrived[:, None, :], 2 * section_id)
        in_use = jnp.arange(CAP)[None, :] < counts[:, block_id:block_id + 1]
        results.append(jnp.where(in_use, slots, -1))
    return jnp.stack(results, axis=1).astype(jnp.int32)


def draw_neighbours(key, part):
    counts = live_counts(key)
    arrived = received_counts(counts)
    kinds = jax.random.randint(jax.random.fold_in(key, 7201), (K, DOMAINS, A_DEV), 0, 8)
    centre = jnp.arange(A_DEV)[None, None, :]
    others = (centre + 1 + jax.random.randint(jax.random.fold_in(key, 7202), (K, DOMAINS, A_DEV), 0, A_DEV - 1)) % A_DEV
    ghost_total = jnp.sum(arrived, axis=1)
    picked = jax.random.randint(jax.random.fold_in(key, 7203), (K, DOMAINS, A_DEV), 0, ghost_total[None, :, None]) + A_DEV
    ghosts = slot_of(picked, arrived[None, :, None, :], 6)
    result = jnp.where(kinds == 0, -1, jnp.where(kinds < 4, others, ghosts))
    return result.reshape(K, ATOMS).astype(jnp.int32)


def block_scale(own_key, shape, split, least, top_value):
    def one(axis_at, parts):
        heights = jax.random.uniform(jax.random.fold_in(jax.random.fold_in(own_key, 6), axis_at), (parts,), jnp.float32, least / len(split), top_value / len(split))
        return jnp.repeat(jnp.exp(heights), shape[axis_at] // parts).reshape((-1,) + (1,) * (len(shape) - axis_at - 1))

    loudness = one(*split[0])
    for cut in split[1:]:
        loudness = loudness * one(*cut)
    return loudness


def noise(stream_key, dims, width, most, shards=(), held_as=jnp.bfloat16):
    drawn = jax.random.normal(stream_key, dims, jnp.float32) * width
    if len(shards) > 0:
        drawn = block_scale(stream_key, dims, shards, -0.22, 0.18) * drawn
    return jnp.clip(drawn, min=-most, max=most).astype(held_as)


def setup_inputs(seed: int = 0) -> dict:
    arg_keys = jax.random.split(jax.random.key(seed), 17)
    positions = jnp.clip(1.0 * jax.random.uniform(arg_keys[0], (3, ATOMS), jnp.float32) ** block_scale(arg_keys[0], (3, ATOMS), ((1, 128),), -0.2, 0.2), 0.0, 1.0)
    send_lists = draw_send_lists(jax.random.fold_in(arg_keys[16], 71), 0)
    neighbours = draw_neighbours(jax.random.fold_in(arg_keys[16], 71), 0)
    emb_scale = noise(arg_keys[3], (MODELS, E1), 1.0, 4.0, ((0, 4),), jnp.float32)
    emb_shift = noise(arg_keys[4], (MODELS, E1), 1.0, 4.0, ((0, 4),), jnp.float32)
    emb_middle = noise(arg_keys[5], (MODELS, E2, E1), E1 ** -0.5, 1.25, ((0, 4),))
    emb_mid_bias = noise(arg_keys[6], (MODELS, E2), 0.5, 3.0, ((0, 4),), jnp.float32)
    emb_outer = noise(arg_keys[7], (MODELS, E3, E2), E2 ** -0.5, 0.875, ((0, 4),))
    emb_out_bias = noise(arg_keys[8], (MODELS, E3), 0.5, 3.0, ((0, 4),), jnp.float32)
    fit_first = noise(arg_keys[9], (MODELS, FIT, E3 * AXIS), (4 * E3 * AXIS) ** -0.5, 0.078125, ((0, 4),))
    fit_first_bias = noise(arg_keys[10], (MODELS, FIT), 0.5, 3.0, ((0, 4),), jnp.float32)
    fit_second = noise(arg_keys[11], (MODELS, FIT, FIT), FIT ** -0.5, 0.375, ((0, 4),))
    fit_second_bias = noise(arg_keys[12], (MODELS, FIT), 0.5, 3.0, ((0, 4),), jnp.float32)
    fit_third = noise(arg_keys[13], (MODELS, FIT, FIT), FIT ** -0.5, 0.375, ((0, 4),))
    fit_third_bias = noise(arg_keys[14], (MODELS, FIT), 0.5, 3.0, ((0, 4),), jnp.float32)
    fit_readout = noise(arg_keys[15], (MODELS, FIT), FIT ** -0.5, 0.375, ((0, 4),))
    return dict(positions=positions, send_lists=send_lists, neighbours=neighbours, emb_scale=emb_scale, emb_shift=emb_shift, emb_middle=emb_middle, emb_mid_bias=emb_mid_bias, emb_outer=emb_outer, emb_out_bias=emb_out_bias, fit_first=fit_first, fit_first_bias=fit_first_bias, fit_second=fit_second, fit_second_bias=fit_second_bias, fit_third=fit_third, fit_third_bias=fit_third_bias, fit_readout=fit_readout)


SOFTEN = 0.04

def describe(pieces, embedding):
    offsets, present = pieces
    scale_in, shift_in, mat_two, bias_two, mat_three, bias_three = embedding
    radius_sq = lax.optimization_barrier(jnp.sum(offsets * offsets, axis=0)) + SOFTEN
    inverse = lax.rsqrt(radius_sq)
    scaled = inverse * inverse
    envelope = jnp.stack([inverse, scaled * offsets[0], scaled * offsets[1], scaled * offsets[2]]) * present[None]
    flat_inv = inverse.reshape(1, -1)
    layer_one = jnp.tanh(scale_in[:, None] * flat_inv + shift_in[:, None]).astype(jnp.bfloat16)
    pre_two = jnp.dot(mat_two, layer_one, preferred_element_type=jnp.float32) + bias_two[:, None]
    layer_two = (jnp.concatenate([layer_one, layer_one], axis=0).astype(jnp.float32) + jnp.tanh(pre_two)).astype(jnp.bfloat16)
    pre_three = jnp.dot(mat_three, layer_two, preferred_element_type=jnp.float32) + bias_three[:, None]
    layer_three = (jnp.concatenate([layer_two, layer_two], axis=0).astype(jnp.float32) + jnp.tanh(pre_three)).astype(jnp.bfloat16)
    filters = layer_three.astype(jnp.float32).reshape(layer_three.shape[0], offsets.shape[1], offsets.shape[2])
    moments = jnp.einsum('ckb,mkb->cmb', envelope, filters, precision=lax.Precision.HIGHEST) / K
    feature = jnp.einsum('cmb,cnb->mnb', moments, moments[:, :AXIS], precision=lax.Precision.HIGHEST)
    return feature.reshape(-1, offsets.shape[2]).astype(jnp.bfloat16)

def domain_energy(offsets, present, embedding, fitting):
    atom_count = offsets.shape[2]
    block_len = 128 if atom_count % 128 == 0 else atom_count
    block_total = atom_count // block_len
    shaped = offsets.reshape(3, K, block_total, block_len).transpose(2, 0, 1, 3)
    present_blocks = present.reshape(K, block_total, block_len).transpose(1, 0, 2)
    features = lax.map(lambda pieces: describe(pieces, embedding), (shaped, present_blocks))
    features = features.transpose(1, 0, 2).reshape(-1, atom_count)
    fit_one, fit_bias_one, fit_two, fit_bias_two, fit_three, fit_bias_three, readout = fitting
    hidden_one = jnp.tanh(jnp.dot(fit_one, features, preferred_element_type=jnp.float32) + fit_bias_one[:, None]).astype(jnp.bfloat16)
    hidden_two = (hidden_one.astype(jnp.float32) + jnp.tanh(jnp.dot(fit_two, hidden_one, preferred_element_type=jnp.float32) + fit_bias_two[:, None])).astype(jnp.bfloat16)
    hidden_three = (hidden_two.astype(jnp.float32) + jnp.tanh(jnp.dot(fit_three, hidden_two, preferred_element_type=jnp.float32) + fit_bias_three[:, None])).astype(jnp.bfloat16)
    return jnp.sum(jnp.dot(readout, hidden_three, preferred_element_type=jnp.float32))

def domain_terms(extended, neighbour_ids, embedding, fitting):
    owned_count = neighbour_ids.shape[1]
    ext_len = extended.shape[1]
    present = neighbour_ids >= 0
    safe_ids = jnp.where(present, neighbour_ids, ext_len)
    gathered = jnp.take(extended, safe_ids, axis=1, mode='fill', fill_value=0.0)
    offsets = gathered - extended[:, None, :owned_count]
    present_f = present.astype(jnp.float32)
    energy, pullback = jax.vjp(lambda shifted: domain_energy(shifted, present_f, embedding, fitting), offsets)
    gradient, = pullback(jnp.ones((), jnp.float32))
    virial = -(offsets[:, None] * gradient[None, :]).reshape(9, K, owned_count)
    spread_terms = jnp.concatenate([-gradient, virial], axis=0).reshape(12, -1)
    totals = jnp.zeros((12, ext_len), jnp.float32).at[:, safe_ids.reshape(-1)].add(spread_terms, mode='drop')
    centre = lax.optimization_barrier(jnp.sum(gradient, axis=1))
    return totals.at[0:3, :owned_count].add(centre)

def pick_columns(extended, chosen):
    safe_ids = jnp.where(chosen >= 0, chosen, extended.shape[1])
    return jnp.take(extended, safe_ids, axis=1, mode='fill', fill_value=0.0)

def add_columns(totals, chosen, values):
    safe_ids = jnp.where(chosen >= 0, chosen, totals.shape[1])
    return totals.at[:, safe_ids].add(values, mode='drop')

def reference(positions, send_lists, neighbours, emb_scale, emb_shift, emb_middle, emb_mid_bias, emb_outer, emb_out_bias, fit_first, fit_first_bias, fit_second, fit_second_bias, fit_third, fit_third_bias, fit_readout):
    strides = (GY * GZ, GZ, 1)
    domain_pos = positions.reshape(3, DOMAINS, A_DEV).transpose(1, 0, 2)
    domain_ids = neighbours.reshape(K, DOMAINS, A_DEV).transpose(1, 0, 2)
    extended = domain_pos
    for section_id in range(3):
        arrived = []
        for side_id in range(2):
            chosen = send_lists[:, 2 * section_id + side_id]
            payload = jax.vmap(pick_columns)(extended, chosen)
            rolled = jnp.roll(payload, strides[section_id] if side_id == 0 else -strides[section_id], axis=0)
            offset_vec = jnp.zeros((1, 3, 1), jnp.float32).at[0, section_id, 0].set(-1.0 if side_id == 0 else 1.0)
            arrived.append(rolled + offset_vec)
        extended = jnp.concatenate([extended] + arrived, axis=2)
    collected = []
    for member in range(MODELS):
        embedding = (emb_scale[member], emb_shift[member], emb_middle[member], emb_mid_bias[member], emb_outer[member], emb_out_bias[member])
        fitting = (fit_first[member], fit_first_bias[member], fit_second[member], fit_second_bias[member], fit_third[member], fit_third_bias[member], fit_readout[member])
        domain_sums = lax.map(lambda pieces: domain_terms(pieces[0], pieces[1], embedding, fitting), (extended, domain_ids))
        for section_id in (2, 1, 0):
            returned = []
            for side_id in range(2):
                first_col = A_DEV + (2 * section_id + side_id) * CAP
                ghost_block = domain_sums[:, :, first_col:first_col + CAP]
                rolled = jnp.roll(ghost_block, -strides[section_id] if side_id == 0 else strides[section_id], axis=0)
                returned.append(rolled)
            for side_id in range(2):
                domain_sums = jax.vmap(add_columns)(domain_sums, send_lists[:, 2 * section_id + side_id], returned[side_id])
        collected.append(domain_sums[:, :, :A_DEV])
    stacked = jnp.stack(collected)
    mean_all = lax.optimization_barrier(jnp.mean(stacked, axis=0))
    deviation = stacked - mean_all[None]
    force_spread = lax.optimization_barrier(jnp.mean(lax.optimization_barrier(jnp.sum(deviation[:, :, 0:3] ** 2, axis=2)), axis=0))
    virial_spread = lax.optimization_barrier(jnp.mean(lax.optimization_barrier(jnp.sum(deviation[:, :, 3:12] ** 2, axis=2)), axis=0))
    mean_force = mean_all[:, 0:3].transpose(1, 0, 2).reshape(3, DOMAINS, MODELS, QUART)
    return (mean_force, force_spread.reshape(DOMAINS, MODELS, QUART), virial_spread.reshape(DOMAINS, MODELS, QUART))
```

```python
import jax
import jax.numpy as jnp
from jax import lax
from jax.experimental import pallas as pl
from jax.experimental.pallas import tpu as pltpu
from jax.sharding import PartitionSpec as P

F32, BF16, I32 = jnp.float32, jnp.bfloat16, jnp.int32
K = 96
ROWS = K // 2
SOFTEN = 0.04
RUN = 8
SPAN = 3
OFFSETS = tuple((a, b, c) for a in (-1, 0, 1) for b in (-1, 0, 1) for c in (-1, 0, 1))


def slot_of(a, b, c):
    return (a + 1) * 9 + (b + 1) * 3 + (c + 1)


def step_of(a, b, c):
    return 16 * a + 4 * b + c


def place_of(a, b, c):
    return (3 if 4 * b + c <= -3 else 0) + a + 1


def iota(shape, dim):
    return lax.broadcasted_iota(I32, shape, dim)


def lanes_of(table, index):
    return jnp.take_along_axis(table, index, axis=1, mode="promise_in_bounds")


def across(row, count):
    return jnp.broadcast_to(row, (count, row.shape[1]))


def half_turn(x):
    return pltpu.roll(x, 64, axis=x.ndim - 1)


def dot(a, b):
    return jnp.dot(a, b, preferred_element_type=F32)


def dot_last(a, b):
    return lax.dot_general(a, b, (((1,), (1,)), ((), ())), preferred_element_type=F32)


def outgoing(lists_ref, pos_ref, out_ref):
    count = out_ref.shape[0]
    me = lax.axis_index("space")
    lists = lists_ref[0].astype(F32)
    pos = pos_ref[...]
    row_xy = jnp.concatenate([pos[0:1], pos[1:2]], axis=1)
    row_z = jnp.concatenate([pos[2:3], pos[2:3]], axis=1)
    for a, b, c in OFFSETS:
        target = lax.rem(me + step_of(a, b, c) + count, count)
        block = next((2 * s + (0 if v > 0 else 1) for s, v in enumerate((a, b, c)) if v), None)
        first = jnp.zeros((1, 128), F32) if block is None else lists[block : block + 1]
        out_ref[target, :, 0:128] = first
        out_ref[target, :, 128:256] = row_xy
        out_ref[target, :, 256:384] = row_z


def grouped(rows, cols, by_row):
    r, c = iota((rows, cols), 0), iota((rows, cols), 1)
    wide, narrow = (r, c) if by_row else (c, r)
    hit = (narrow == (wide // 32) * 25 + wide % 32) & (wide % 32 < 25)
    return hit.astype(F32).astype(BF16)


def eye(n):
    return (iota((n, n), 0) == iota((n, n), 1)).astype(F32).astype(BF16)


def weights(
    scale_ref, shift_ref, mid_ref, mid_b_ref, outer_ref, outer_b_ref,
    one_ref, one_b_ref, two_ref, two_b_ref, three_ref, three_b_ref, read_ref,
    w2_ref, w2t_ref, w3_ref, w3t_ref, cols_ref, ecols_ref, f1_ref, f1t_ref, f2t_ref, f3t_ref,
    stack_ref,
):
    w2 = dot(dot(grouped(64, 50, True), mid_ref[0]).astype(BF16), grouped(25, 32, False)).astype(BF16)
    w3 = dot(dot(grouped(128, 100, True), outer_ref[0]).astype(BF16), grouped(50, 64, False)).astype(BF16)
    w2_ref[...] = w2
    w3_ref[...] = w3
    w2t_ref[...] = dot_last(eye(32), w2).astype(BF16)
    w3t_ref[...] = dot_last(eye(64), w3).astype(BF16)
    f2t_ref[...] = dot_last(eye(240), two_ref[0]).astype(BF16)
    f3t_ref[...] = dot_last(eye(240), three_ref[0]).astype(BF16)
    stack_ref[...] = jnp.zeros_like(stack_ref)
    small = (scale_ref, shift_ref, mid_b_ref, outer_b_ref, one_b_ref, two_b_ref, three_b_ref, read_ref)
    for i, ref in enumerate(small):
        stack_ref[i : i + 1, 0 : ref.shape[1]] = ref[...].astype(F32)
    turned = jnp.transpose(stack_ref[...], (1, 0))
    cols_ref[...] = turned
    ecols_ref[...] = jnp.zeros_like(ecols_ref)
    for q in range(4):
        ecols_ref[32 * q : 32 * q + 25, :] = turned[25 * q : 25 * q + 25]
    f1t_ref[...] = jnp.zeros_like(f1t_ref)
    for part in range(2):
        r, c = iota((256, 128), 0), iota((256, 128), 1)
        pick = (r == (c % 16) * 16 + c // 16 + 8 * part).astype(F32).astype(BF16)
        r, c = iota((128, 256), 0), iota((128, 256), 1)
        pick_t = (c == (r % 16) * 16 + r // 16 + 8 * part).astype(F32).astype(BF16)
        for blk in range(7):
            wide = min(256, 1600 - 256 * blk)
            piece = one_ref[0, :, 256 * blk : 256 * blk + wide]
            f1_ref[240 * part : 240 * part + 240, 128 * blk : 128 * blk + 128] = dot(
                piece, pick[0:wide]
            ).astype(BF16)
            f1t_ref[128 * blk : 128 * blk + 128, 256 * part : 256 * part + 240] = dot_last(
                pick_t[:, 0:wide], piece
            ).astype(BF16)


def resolve(me, count, recv_ref, num_ref, ext_ref, code_ref):
    def source(a, b, c):
        return lax.rem(me - step_of(a, b, c) + count, count)

    def listed(a, b, c):
        return recv_ref[source(a, b, c), :, 0:128].astype(I32)

    def coded(a, b, c):
        return listed(a, b, c) + 64 * slot_of(a, b, c)

    num_ref[...] = jnp.zeros_like(num_ref)
    pairs = [(b, c) for b in (1, -1) for c in (-1, 0, 1)]
    for i, (b, c) in enumerate(pairs):
        entry = listed(0, b, c)
        num_ref[0, i : i + 1] = entry
        num_ref[1, i : i + 1] = entry + 64 * slot_of(0, b, c)
        num_ref[2, i : i + 1] = coded(1, b, c)
        num_ref[3, i : i + 1] = coded(-1, b, c)
    entry = num_ref[0]
    index = (entry + 64) & 127
    middle = jnp.where(
        entry < 64,
        num_ref[1],
        jnp.where(entry < 192, lanes_of(num_ref[2], index), lanes_of(num_ref[3], index)),
    )
    num_ref[4] = middle
    for i, c in enumerate((1, -1)):
        entry = listed(0, 0, c)
        num_ref[5, i : i + 1] = entry
        num_ref[6, i : i + 1] = entry + 64 * slot_of(0, 0, c)
        num_ref[7, i : i + 1] = coded(1, 0, c)
        num_ref[8, i : i + 1] = coded(-1, 0, c)
        num_ref[9, i : i + 1] = num_ref[4, c + 1 : c + 2]
        num_ref[10, i : i + 1] = num_ref[4, c + 4 : c + 5]
    entry = num_ref[5]
    index = (entry + 64) & 127
    found = num_ref[6]
    for i, least in enumerate((64, 192, 320, 448)):
        found = jnp.where(entry < least, found, lanes_of(num_ref[7 + i], index))
    num_ref[11] = found
    code_ref[0:1] = 64 * slot_of(0, 0, 0) + (iota((1, 128), 1) & 63)
    code_ref[1:2] = coded(1, 0, 0)
    code_ref[2:3] = coded(-1, 0, 0)
    code_ref[3:4] = num_ref[4, 1:2]
    code_ref[4:5] = num_ref[4, 4:5]
    code_ref[5:7] = num_ref[11, 0:2]
    code_ref[7:8] = jnp.zeros((1, 128), I32)
    code = code_ref[...]
    atom = code & 63
    owner = code >> 6
    spots = [jnp.zeros((8, 128), F32)] * 3
    for a, b, c in OFFSETS:
        e = source(a, b, c)
        row_xy = across(recv_ref[e, :, 128:256], 8)
        row_z = across(recv_ref[e, :, 256:384], 8)
        here = owner == slot_of(a, b, c)
        got = (lanes_of(row_xy, atom), lanes_of(row_xy, atom + 64), lanes_of(row_z, atom))
        spots = [jnp.where(here, g - float(o), s) for g, o, s in zip(got, (a, b, c), spots)]
    for i in range(3):
        ext_ref[i] = spots[i]


def evaluate(
    recv_ref, nb_ref, w2_ref, w2t_ref, w3_ref, w3t_ref, cols_ref, ecols_ref,
    f1_ref, f1t_ref, f2_ref, f2t_ref, f3_ref, f3t_ref,
    out_ref,
    num_ref, ext_ref, code_ref, idx_ref, off_ref, inv_ref, env_ref, hi_ref, lo_ref,
    s1_ref, s2_ref, s3_ref, h3_ref, mom_ref, nat_ref, axis_ref, feat_ref, dfeat_ref,
    dnat_ref, dmom_ref, denv_ref, dinv_ref, grad_ref, acc_ref,
):
    count = recv_ref.shape[0]
    me = lax.axis_index("space")
    resolve(me, count, recv_ref, num_ref, ext_ref, code_ref)

    idx_ref[:, 0:64] = nb_ref[0:ROWS, :]
    idx_ref[:, 64:128] = nb_ref[ROWS:K, :]
    for q in range(ROWS // 8):
        at = slice(8 * q, 8 * q + 8)
        ids = idx_ref[at]
        present = jnp.where(ids >= 0, 1.0, 0.0)
        row, lane = (ids + 64) >> 7, (ids + 64) & 127
        spots = [jnp.zeros((8, 128), F32)] * 3
        code = jnp.zeros((8, 128), I32)
        for k in range(7):
            here = row == k
            spots = [
                jnp.where(here, lanes_of(across(ext_ref[i, k : k + 1], 8), lane), s)
                for i, s in enumerate(spots)
            ]
            code = jnp.where(here, lanes_of(across(code_ref[k : k + 1], 8), lane), code)
        offs = [s - ext_ref[i, 0:1] for i, s in enumerate(spots)]
        inverse = lax.rsqrt(offs[0] * offs[0] + offs[1] * offs[1] + offs[2] * offs[2] + SOFTEN)
        inv_ref[at] = inverse
        env_ref[0, at] = inverse * present
        for i in range(3):
            off_ref[i, at] = offs[i]
            env_ref[i + 1, at] = (inverse * inverse) * offs[i] * present
        hi_ref[at] = jnp.where(ids >= 0, code >> 7, -1)
        lo_ref[at] = code & 127

    mom_ref[...] = jnp.zeros_like(mom_ref)
    scale = jnp.broadcast_to(ecols_ref[0:32, 0:1], (32, 128))
    shift = jnp.broadcast_to(ecols_ref[0:32, 1:2], (32, 128))
    bias_two = jnp.concatenate([jnp.broadcast_to(ecols_ref[0:64, 2:3], (64, 128))] * 8, axis=1)
    bias_three = jnp.concatenate([jnp.broadcast_to(ecols_ref[0:128, 3:4], (128, 128))] * 8, axis=1)

    def forward(q, carry):
        base = pl.multiple_of(q * 8, 8)
        firsts = []
        for r in range(8):
            t = jnp.tanh(scale * inv_ref[pl.ds(base + r, 1), :] + shift)
            s1_ref[base + r] = (1.0 - t * t).astype(BF16)
            firsts.append(t.astype(BF16))
        h1 = jnp.concatenate(firsts, axis=1)
        t2 = jnp.tanh(dot(w2_ref[...], h1) + bias_two)
        h2 = (jnp.concatenate([h1, h1], axis=0).astype(F32) + t2).astype(BF16)
        s2 = (1.0 - t2 * t2).astype(BF16)
        t3 = jnp.tanh(dot(w3_ref[...], h2) + bias_three)
        h3 = (jnp.concatenate([h2, h2], axis=0).astype(F32) + t3).astype(BF16)
        s3 = (1.0 - t3 * t3).astype(BF16)
        for r in range(8):
            part = slice(128 * r, 128 * r + 128)
            s2_ref[base + r] = s2[:, part]
            s3_ref[base + r] = s3[:, part]
            h3_ref[base + r] = h3[:, part]
        for n in range(8):
            rows = slice(16 * n, 16 * n + 16)
            tiles = [h3[rows, 128 * r : 128 * r + 128].astype(F32) for r in range(8)]
            for c in range(4):
                total = tiles[0] * env_ref[c, pl.ds(base, 1), :]
                for r in range(1, 8):
                    total = total + tiles[r] * env_ref[c, pl.ds(base + r, 1), :]
                mom_ref[c, rows] = mom_ref[c, rows] + total
        return carry

    lax.fori_loop(0, ROWS // 8, forward, 0)

    low = iota((1, 128), 1) < 64
    nat_ref[:, 96:112, :] = jnp.zeros((4, 16, 128), F32)
    for c in range(4):
        m = mom_ref[c]
        m = (m + half_turn(m)) * (1.0 / K)
        for q in range(4):
            nat_ref[c, 25 * q : 25 * q + 25] = m[32 * q : 32 * q + 25]
        axis_ref[c] = jnp.where(low, m[0:8], m[8:16])
    for blk in range(7):
        mine = [nat_ref[c, 16 * blk : 16 * blk + 16] for c in range(4)]
        for p in range(8):
            total = mine[0] * axis_ref[0, p : p + 1]
            for c in range(1, 4):
                total = total + mine[c] * axis_ref[c, p : p + 1]
            feat_ref[128 * blk + 16 * p : 128 * blk + 16 * p + 16] = total.astype(BF16)

    both = dot(f1_ref[...], feat_ref[...])
    pre = jnp.where(low, both[0:240], both[240:480])
    t1 = jnp.tanh(pre + half_turn(pre) + cols_ref[0:240, 4:5])
    g1 = t1.astype(BF16)
    t2 = jnp.tanh(dot(f2_ref[0], g1) + cols_ref[0:240, 5:6])
    g2 = (g1.astype(F32) + t2).astype(BF16)
    t3 = jnp.tanh(dot(f3_ref[0], g2) + cols_ref[0:240, 6:7])
    d3 = jnp.broadcast_to(cols_ref[0:240, 7:8], (240, 128))
    back = dot(f3t_ref[...], (d3 * (1.0 - t3 * t3)).astype(BF16)).astype(BF16).astype(F32)
    d2 = (back + d3).astype(BF16).astype(F32)
    back = dot(f2t_ref[...], (d2 * (1.0 - t2 * t2)).astype(BF16)).astype(BF16).astype(F32)
    d1 = (back + d2).astype(BF16).astype(F32)
    d1 = d1 * (1.0 - t1 * t1)
    none = jnp.zeros((16, 128), F32)
    split = jnp.concatenate([jnp.where(low, d1, 0.0), none, jnp.where(low, 0.0, d1), none], axis=0)
    dfeat_ref[...] = dot(f1t_ref[...], split.astype(BF16)).astype(BF16).astype(F32)

    dmom_ref[...] = jnp.zeros_like(dmom_ref)
    for c in range(4):
        sums = [jnp.zeros((16, 128), F32)] * 8
        for blk in range(7):
            mine = nat_ref[c, 16 * blk : 16 * blk + 16]
            total = jnp.zeros((16, 128), F32)
            for p in range(8):
                d = dfeat_ref[128 * blk + 16 * p : 128 * blk + 16 * p + 16]
                total = total + d * axis_ref[c, p : p + 1]
                sums[p] = sums[p] + d * mine
            dnat_ref[c, 16 * blk : 16 * blk + 16] = total + half_turn(total)
        rows = jnp.concatenate([jnp.sum(s, axis=0, keepdims=True) for s in sums], axis=0)
        turned = half_turn(rows)
        dnat_ref[c, 0:8] = dnat_ref[c, 0:8] + jnp.where(low, rows, turned)
        dnat_ref[c, 8:16] = dnat_ref[c, 8:16] + jnp.where(low, turned, rows)
        for q in range(4):
            dmom_ref[c, 32 * q : 32 * q + 25] = dnat_ref[c, 25 * q : 25 * q + 25] * (1.0 / K)

    def backward(q, carry):
        base = pl.multiple_of(q * 8, 8)
        outer, pushed = [], []
        for r in range(8):
            env = [env_ref[c, pl.ds(base + r, 1), :] for c in range(4)]
            parts = [jnp.zeros((16, 128), F32)] * 4
            tiles = []
            for n in range(8):
                rows = slice(16 * n, 16 * n + 16)
                dm = [dmom_ref[c, rows] for c in range(4)]
                tiles.append((dm[0] * env[0] + dm[1] * env[1] + dm[2] * env[2] + dm[3] * env[3]).astype(BF16))
                h = h3_ref[base + r, rows].astype(F32)
                parts = [s + dm[c] * h for c, s in enumerate(parts)]
            for c in range(4):
                denv_ref[c, pl.ds(base + r, 1), :] = jnp.sum(parts[c], axis=0, keepdims=True)
            d = jnp.concatenate(tiles, axis=0)
            outer.append(d)
            pushed.append((d.astype(F32) * s3_ref[base + r].astype(F32)).astype(BF16))
        d3 = jnp.concatenate(outer, axis=1)
        back = dot(w3t_ref[...], jnp.concatenate(pushed, axis=1)).astype(BF16).astype(F32)
        d2 = (back + d3[0:64].astype(F32) + d3[64:128].astype(F32)).astype(BF16)
        s2 = jnp.concatenate([s2_ref[base + r] for r in range(8)], axis=1)
        back = dot(w2t_ref[...], (d2.astype(F32) * s2.astype(F32)).astype(BF16)).astype(BF16).astype(F32)
        d1 = (back + d2[0:32].astype(F32) + d2[32:64].astype(F32)).astype(BF16).astype(F32)
        for r in range(8):
            d = d1[:, 128 * r : 128 * r + 128] * s1_ref[base + r].astype(F32) * scale
            dinv_ref[pl.ds(base + r, 1), :] = jnp.sum(d, axis=0, keepdims=True)
        return carry

    lax.fori_loop(0, ROWS // 8, backward, 0)

    centre = [jnp.zeros((8, 128), F32)] * 3
    for q in range(ROWS // 8):
        at = slice(8 * q, 8 * q + 8)
        inverse = inv_ref[at]
        present = jnp.where(idx_ref[at] >= 0, 1.0, 0.0)
        offs = [off_ref[i, at] for i in range(3)]
        denv = [denv_ref[c, at] * present for c in range(4)]
        along = denv[1] * offs[0] + denv[2] * offs[1] + denv[3] * offs[2]
        square = inverse * inverse
        slope = (dinv_ref[at] + denv[0] + 2.0 * inverse * along) * (square * inverse) * -1.0
        for i in range(3):
            g = denv[i + 1] * square + slope * offs[i]
            grad_ref[i, at] = g
            centre[i] = centre[i] + g

    acc_ref[...] = jnp.zeros_like(acc_ref)
    which = iota((8, 128), 0)
    lead, next_up, rest = which % 3 == 0, which % 3 == 1, which >= 6
    spot = iota((128, 128), 0)

    def scatter(q, carry):
        base = pl.multiple_of(q * 8, 8)
        left, right = [], []
        for r in range(8):
            at = pl.ds(base + r, 1)
            gx, gy, gz = (across(grad_ref[i, at, :], 8) for i in range(3))
            ox, oy, oz = (across(off_ref[i, at, :], 8) for i in range(3))
            g_even = jnp.where(lead, gx, jnp.where(next_up, gz, gy))
            o_even = jnp.where((which < 2) | rest, 1.0, jnp.where(which == 2, ox, jnp.where(which < 5, oy, oz)))
            g_odd = jnp.where(lead, gy, jnp.where(next_up, gx, gz))
            o_odd = jnp.where((which < 1) | rest, 1.0, jnp.where(which < 3, ox, jnp.where(which < 4, oy, oz)))
            halves = (-g_even * o_even, -g_odd * o_odd)
            term = jnp.concatenate([jnp.where(rest, t - t.astype(BF16).astype(F32), t) for t in halves], axis=0)
            high = across(hi_ref[at, :], 16)
            left.append(jnp.concatenate([jnp.where(high == h, term, 0.0).astype(BF16) for h in range(14)], axis=0))
            right.append(jnp.where(spot == lo_ref[at, :], 1.0, 0.0).astype(BF16))
        acc_ref[...] = acc_ref[...] + dot_last(jnp.concatenate(left, axis=1), jnp.concatenate(right, axis=1))
        return carry

    lax.fori_loop(0, ROWS // 8, scatter, 0)

    rows = [jnp.sum(s, axis=0, keepdims=True) for s in centre]
    rows = [s + half_turn(s) for s in rows]
    own = jnp.concatenate(
        [jnp.where(low, rows[0], rows[1]), jnp.where(low, rows[2], 0.0), jnp.zeros((6, 128), F32)], axis=0
    )
    mine = me & (RUN - 1)
    for a, b, c in OFFSETS:
        h, odd = divmod(slot_of(a, b, c), 2)
        even_terms = acc_ref[16 * h : 16 * h + 8]
        odd_terms = acc_ref[16 * h + 8 : 16 * h + 16]
        even_terms = even_terms + jnp.where(which < 2, pltpu.roll(even_terms, 2, axis=0), 0.0)
        odd_terms = odd_terms + jnp.where(which < 1, pltpu.roll(odd_terms, 2, axis=0), 0.0)
        if odd:
            tile = jnp.where(low, half_turn(even_terms), odd_terms)
        else:
            tile = jnp.where(low, even_terms, half_turn(odd_terms))
        if (a, b, c) == (0, 0, 0):
            tile = tile + own
        place = 8 * place_of(a, b, c)
        out_ref[(mine - (4 * b + c)) & (RUN - 1), place : place + 8, :] = tile


def regroup(recv_ref, out_ref, sum_ref):
    me = lax.axis_index("space")
    mine, run = me & (RUN - 1), me // RUN
    runs = out_ref.shape[0] // 4
    sum_ref[...] = jnp.zeros_like(sum_ref)
    for a, b, c in OFFSETS:
        moved = mine + 4 * b + c
        away = pl.multiple_of(8 * (SPAN - 2 * a - (moved >> 3)), 8)
        place = 8 * place_of(a, b, c)
        sum_ref[pl.ds(away, 8), :] = sum_ref[pl.ds(away, 8), :] + recv_ref[moved & (RUN - 1), place : place + 8, :]
    parts = [sum_ref[pl.ds(k, 8, stride=8), :] for k in range(6)]
    lane = iota((8, 128), 1) // 16
    for quarter in range(4):
        for side in range(2):
            total = jnp.zeros((8, 128), F32)
            for k in range(6):
                turn = (16 * k - 64 * side - 16 * quarter) % 128
                piece = parts[k] if turn == 0 else pltpu.roll(parts[k], turn, axis=1)
                total = jnp.where(lane == k, piece, total)
            for o in range(2 * SPAN + 1):
                target = quarter * runs + ((run + o - SPAN) & (runs - 1))
                out_ref[target, :, 128 * side : 128 * side + 128] = total[o : o + 1]


def finish(recv_ref, mean_ref, force_ref, virial_ref):
    run = lax.axis_index("space") // RUN
    runs = recv_ref.shape[0] // 4
    totals = []
    for m in range(4):
        total = recv_ref[m * runs + run]
        for o in range(-SPAN, SPAN + 1):
            if o != 0:
                total = total + recv_ref[m * runs + ((run - o) & (runs - 1))]
        totals.append(total)
    mean = (totals[0] + totals[1] + totals[2] + totals[3]) * 0.25
    spread = jnp.zeros_like(mean)
    for total in totals:
        spread = spread + (total - mean) * (total - mean)
    spread = spread * 0.25

    def component(x, k):
        half = x[:, 128 * (k % 2) : 128 * (k % 2) + 128]
        turn = (-16 * (k // 2)) % 128
        return half if turn == 0 else pltpu.roll(half, turn, axis=1)

    for k in range(3):
        mean_ref[k, 0] = component(mean, k)[:, 0:16]
    force = component(spread, 0)
    for k in range(1, 3):
        force = force + component(spread, k)
    force_ref[0] = force[:, 0:16]
    virial = component(spread, 3)
    for k in range(4, 12):
        virial = virial + component(spread, k)
    virial_ref[0] = virial[:, 0:16]


def call(body, out_shape, scratch=(), limit=16 << 20, cost=None):
    return pl.pallas_call(
        body,
        out_shape=out_shape,
        scratch_shapes=list(scratch),
        compiler_params=pltpu.CompilerParams(vmem_limit_bytes=limit),
        cost_estimate=cost,
    )


def shaped(shape, dtype=F32):
    return jax.ShapeDtypeStruct(shape, dtype)


def local(
    positions, send_lists, neighbours,
    emb_scale, emb_shift, emb_middle, emb_mid_bias, emb_outer, emb_out_bias,
    fit_first, fit_first_bias, fit_second, fit_second_bias, fit_third, fit_third_bias, fit_readout,
):
    count = lax.axis_size("space")
    models = lax.axis_size("mp")
    runs = count // RUN
    packed = call(outgoing, shaped((count, 1, 384)))(send_lists, positions)
    arrived = lax.all_to_all(packed, "space", 0, 0)
    w2, w2t, w3, w3t, cols, ecols, f1, f1t, f2t, f3t = call(
        weights,
        (
            shaped((64, 32), BF16), shaped((32, 64), BF16), shaped((128, 64), BF16), shaped((64, 128), BF16),
            shaped((256, 128)), shaped((128, 128)), shaped((480, 896), BF16), shaped((896, 512), BF16),
            shaped((240, 240), BF16), shaped((240, 240), BF16),
        ),
        [pltpu.VMEM((128, 256), F32)],
    )(
        emb_scale, emb_shift, emb_middle, emb_mid_bias, emb_outer, emb_out_bias,
        fit_first, fit_first_bias, fit_second, fit_second_bias, fit_third, fit_third_bias, fit_readout,
    )
    pair = (ROWS, 128)
    terms = call(
        evaluate,
        shaped((RUN, 48, 128)),
        [
            pltpu.VMEM((12, 8, 128), I32), pltpu.VMEM((3, 8, 128), F32), pltpu.VMEM((8, 128), I32),
            pltpu.VMEM(pair, I32), pltpu.VMEM((3, *pair), F32), pltpu.VMEM(pair, F32), pltpu.VMEM((4, *pair), F32),
            pltpu.VMEM(pair, I32), pltpu.VMEM(pair, I32),
            pltpu.VMEM((ROWS, 32, 128), BF16), pltpu.VMEM((ROWS, 64, 128), BF16),
            pltpu.VMEM((ROWS, 128, 128), BF16), pltpu.VMEM((ROWS, 128, 128), BF16),
            pltpu.VMEM((4, 128, 128), F32), pltpu.VMEM((4, 112, 128), F32), pltpu.VMEM((4, 8, 128), F32),
            pltpu.VMEM((896, 128), BF16), pltpu.VMEM((896, 128), F32),
            pltpu.VMEM((4, 112, 128), F32), pltpu.VMEM((4, 128, 128), F32),
            pltpu.VMEM((4, *pair), F32), pltpu.VMEM(pair, F32), pltpu.VMEM((3, *pair), F32),
            pltpu.VMEM((224, 128), F32),
        ],
        32 << 20,
    )(arrived, neighbours, w2, w2t, w3, w3t, cols, ecols, f1, f1t, fit_second, f2t, fit_third, f3t)
    near = [[RUN * u + v for v in range(RUN)] for u in range(runs)]
    terms = lax.all_to_all(terms, "space", 0, 0, axis_index_groups=near)
    terms = call(regroup, shaped((models * runs, 1, 256)), [pltpu.VMEM((64, 128), F32)])(terms)
    far = [[m * count + RUN * u + v for m in range(models) for u in range(runs)] for v in range(RUN)]
    terms = lax.all_to_all(terms, ("mp", "space"), 0, 0, axis_index_groups=far)
    quarter = positions.shape[1] // models
    return call(
        finish, (shaped((3, 1, 1, quarter)), shaped((1, 1, quarter)), shaped((1, 1, quarter)))
    )(terms)


def solution(mesh):
    params = [P("mp", None)] * 2 + [P("mp", None, None), P("mp", None)] * 5 + [P("mp", None)]
    return jax.shard_map(
        local,
        mesh=mesh,
        in_specs=(P(None, "space"), P("space", None, None), P(None, "space"), *params),
        out_specs=(P(None, "space", "mp", None), P("space", "mp", None), P("space", "mp", None)),
        check_vma=False,
    )
```

```python
import jax
import jax.numpy as jnp
from jax import lax
from jax.experimental import pallas as pl
from jax.experimental.pallas import tpu as pltpu
from jax.sharding import PartitionSpec as P

F32, BF16, I32 = jnp.float32, jnp.bfloat16, jnp.int32
K = 96
ROWS = K // 2
SOFTEN = 0.04
RUN = 8
SPAN = 3
OFFSETS = tuple((a, b, c) for a in (-1, 0, 1) for b in (-1, 0, 1) for c in (-1, 0, 1))


def slot_of(a, b, c):
    return (a + 1) * 9 + (b + 1) * 3 + (c + 1)


def step_of(a, b, c):
    return 16 * a + 4 * b + c


def place_of(a, b, c):
    return (3 if 4 * b + c <= -3 else 0) + a + 1


def iota(shape, dim):
    return lax.broadcasted_iota(I32, shape, dim)


def lanes_of(table, index):
    return jnp.take_along_axis(table, index, axis=1, mode="promise_in_bounds")


def across(row, count):
    return jnp.broadcast_to(row, (count, row.shape[1]))


def half_turn(x):
    return pltpu.roll(x, 64, axis=x.ndim - 1)


def dot(a, b):
    return jnp.dot(a, b, preferred_element_type=F32)


def dot_last(a, b):
    return lax.dot_general(a, b, (((1,), (1,)), ((), ())), preferred_element_type=F32)


def outgoing(lists_hbm, pos_hbm, out_ref, lists_ref, pos_ref, sems):
    fetches = [
        pltpu.make_async_copy(lists_hbm, lists_ref, sems.at[0]),
        pltpu.make_async_copy(pos_hbm, pos_ref, sems.at[1]),
    ]
    for fetch in fetches:
        fetch.start()
    for fetch in fetches:
        fetch.wait()
    count = out_ref.shape[0]
    me = lax.axis_index("space")
    lists = lists_ref[:, 0, :].astype(F32)
    pos = pos_ref[...]
    row_xy = jnp.concatenate([pos[0:1], pos[1:2]], axis=1)
    row_z = jnp.concatenate([pos[2:3], pos[2:3]], axis=1)
    for a, b, c in OFFSETS:
        target = lax.rem(me + step_of(a, b, c) + count, count)
        block = next((2 * s + (0 if v > 0 else 1) for s, v in enumerate((a, b, c)) if v), None)
        first = jnp.zeros((1, 128), F32) if block is None else lists[block : block + 1]
        out_ref[target, :, 0:128] = first
        out_ref[target, :, 128:256] = row_xy
        out_ref[target, :, 256:384] = row_z


def grouped(rows, cols, by_row):
    r, c = iota((rows, cols), 0), iota((rows, cols), 1)
    wide, narrow = (r, c) if by_row else (c, r)
    hit = (narrow == (wide // 32) * 25 + wide % 32) & (wide % 32 < 25)
    return hit.astype(F32).astype(BF16)


def eye(n):
    return (iota((n, n), 0) == iota((n, n), 1)).astype(F32).astype(BF16)


def weights(
    scale_ref, shift_ref, mid_ref, mid_b_ref, outer_ref, outer_b_ref,
    one_ref, one_b_ref, two_ref, two_b_ref, three_ref, three_b_ref, read_ref,
    w2_ref, w2t_ref, w3_ref, w3t_ref, cols_ref, ecols_ref, f1_ref, f1t_ref, f2t_ref, f3t_ref,
    stack_ref,
):
    w2 = dot(dot(grouped(64, 50, True), mid_ref[0]).astype(BF16), grouped(25, 32, False)).astype(BF16)
    w3 = dot(dot(grouped(128, 100, True), outer_ref[0]).astype(BF16), grouped(50, 64, False)).astype(BF16)
    w2t_ref[...] = dot_last(eye(32), w2).astype(BF16)
    w3t_ref[...] = dot_last(eye(64), w3).astype(BF16)
    f2t_ref[...] = dot_last(eye(240), two_ref[0]).astype(BF16)
    f3t_ref[...] = dot_last(eye(240), three_ref[0]).astype(BF16)
    stack_ref[...] = jnp.zeros_like(stack_ref)
    small = (scale_ref, shift_ref, mid_b_ref, outer_b_ref, one_b_ref, two_b_ref, three_b_ref, read_ref)
    for i, ref in enumerate(small):
        stack_ref[i : i + 1, 0 : ref.shape[1]] = ref[...].astype(F32)
    turned = jnp.transpose(stack_ref[...], (1, 0))
    cols_ref[...] = turned
    ecols_ref[...] = jnp.zeros_like(ecols_ref)
    for q in range(4):
        ecols_ref[32 * q : 32 * q + 25, :] = turned[25 * q : 25 * q + 25]
    for w, ref, column in ((w2, w2_ref, 2), (w3, w3_ref, 3)):
        bias = jnp.broadcast_to(ecols_ref[0 : w.shape[0], column : column + 1], w.shape)
        whole = bias.astype(BF16).astype(F32)
        lane = iota(w.shape, 1)
        ref[...] = jnp.where(lane == 25, whole, jnp.where(lane == 26, bias - whole, w.astype(F32))).astype(BF16)
    f1t_ref[...] = jnp.zeros_like(f1t_ref)
    for part in range(2):
        r, c = iota((256, 128), 0), iota((256, 128), 1)
        pick = (r == (c % 16) * 16 + c // 16 + 8 * part).astype(F32).astype(BF16)
        r, c = iota((128, 256), 0), iota((128, 256), 1)
        pick_t = (c == (r % 16) * 16 + r // 16 + 8 * part).astype(F32).astype(BF16)
        for blk in range(7):
            wide = min(256, 1600 - 256 * blk)
            piece = one_ref[0, :, 256 * blk : 256 * blk + wide]
            f1_ref[240 * part : 240 * part + 240, 128 * blk : 128 * blk + 128] = dot(
                piece, pick[0:wide]
            ).astype(BF16)
            f1t_ref[128 * blk : 128 * blk + 128, 256 * part : 256 * part + 240] = dot_last(
                pick_t[:, 0:wide], piece
            ).astype(BF16)


def resolve(me, count, recv_ref, num_ref, ext_ref, code_ref):
    def source(a, b, c):
        return lax.rem(me - step_of(a, b, c) + count, count)

    def listed(a, b, c):
        return recv_ref[source(a, b, c), :, 0:128].astype(I32)

    def coded(a, b, c):
        return listed(a, b, c) + 64 * slot_of(a, b, c)

    num_ref[...] = jnp.zeros_like(num_ref)
    pairs = [(b, c) for b in (1, -1) for c in (-1, 0, 1)]
    for i, (b, c) in enumerate(pairs):
        entry = listed(0, b, c)
        num_ref[0, i : i + 1] = entry
        num_ref[1, i : i + 1] = entry + 64 * slot_of(0, b, c)
        num_ref[2, i : i + 1] = coded(1, b, c)
        num_ref[3, i : i + 1] = coded(-1, b, c)
    entry = num_ref[0]
    index = (entry + 64) & 127
    middle = jnp.where(
        entry < 64,
        num_ref[1],
        jnp.where(entry < 192, lanes_of(num_ref[2], index), lanes_of(num_ref[3], index)),
    )
    num_ref[4] = middle
    for i, c in enumerate((1, -1)):
        entry = listed(0, 0, c)
        num_ref[5, i : i + 1] = entry
        num_ref[6, i : i + 1] = entry + 64 * slot_of(0, 0, c)
        num_ref[7, i : i + 1] = coded(1, 0, c)
        num_ref[8, i : i + 1] = coded(-1, 0, c)
        num_ref[9, i : i + 1] = num_ref[4, c + 1 : c + 2]
        num_ref[10, i : i + 1] = num_ref[4, c + 4 : c + 5]
    entry = num_ref[5]
    index = (entry + 64) & 127
    found = num_ref[6]
    for i, least in enumerate((64, 192, 320, 448)):
        found = jnp.where(entry < least, found, lanes_of(num_ref[7 + i], index))
    num_ref[11] = found
    code_ref[0:1] = 64 * slot_of(0, 0, 0) + (iota((1, 128), 1) & 63)
    code_ref[1:2] = coded(1, 0, 0)
    code_ref[2:3] = coded(-1, 0, 0)
    code_ref[3:4] = num_ref[4, 1:2]
    code_ref[4:5] = num_ref[4, 4:5]
    code_ref[5:7] = num_ref[11, 0:2]
    code_ref[7:8] = jnp.zeros((1, 128), I32)
    code = code_ref[...]
    atom = code & 63
    owner = code >> 6
    spots = [jnp.zeros((8, 128), F32)] * 3
    for a, b, c in OFFSETS:
        e = source(a, b, c)
        row_xy = across(recv_ref[e, :, 128:256], 8)
        row_z = across(recv_ref[e, :, 256:384], 8)
        here = owner == slot_of(a, b, c)
        got = (lanes_of(row_xy, atom), lanes_of(row_xy, atom + 64), lanes_of(row_z, atom))
        spots = [jnp.where(here, g - float(o), s) for g, o, s in zip(got, (a, b, c), spots)]
    for i in range(3):
        ext_ref[i] = spots[i]


def evaluate(
    recv_ref, nb_ref, w2_ref, w2t_ref, w3_ref, w3t_ref, cols_ref, ecols_ref,
    f1_ref, f1t_ref, f2_ref, f2t_ref, f3_ref, f3t_ref,
    out_ref,
    num_ref, ext_ref, code_ref, idx_ref, off_ref, inv_ref, env_ref, hi_ref, lo_ref,
    s1_ref, s2_ref, s3_ref, h3_ref, mom_ref, nat_ref, axis_ref, feat_ref, dfeat_ref,
    dnat_ref, denv_ref, dinv_ref, grad_ref, acc_ref,
):
    count = recv_ref.shape[0]
    me = lax.axis_index("space")
    resolve(me, count, recv_ref, num_ref, ext_ref, code_ref)

    idx_ref[:, 0:64] = nb_ref[0:ROWS, :]
    idx_ref[:, 64:128] = nb_ref[ROWS:K, :]
    for q in range(ROWS // 8):
        at = slice(8 * q, 8 * q + 8)
        ids = idx_ref[at]
        present = jnp.where(ids >= 0, 1.0, 0.0)
        row, lane = (ids + 64) >> 7, (ids + 64) & 127
        spots = [jnp.zeros((8, 128), F32)] * 3
        code = jnp.zeros((8, 128), I32)
        for k in range(7):
            here = row == k
            spots = [
                jnp.where(here, lanes_of(across(ext_ref[i, k : k + 1], 8), lane), s)
                for i, s in enumerate(spots)
            ]
            code = jnp.where(here, lanes_of(across(code_ref[k : k + 1], 8), lane), code)
        offs = [s - ext_ref[i, 0:1] for i, s in enumerate(spots)]
        inverse = lax.rsqrt(offs[0] * offs[0] + offs[1] * offs[1] + offs[2] * offs[2] + SOFTEN)
        inv_ref[at] = inverse
        env_ref[0, at] = inverse * present
        for i in range(3):
            off_ref[i, at] = offs[i]
            env_ref[i + 1, at] = (inverse * inverse) * offs[i] * present
        hi_ref[at] = jnp.where(ids >= 0, code >> 7, -1)
        lo_ref[at] = code & 127

    mom_ref[...] = jnp.zeros_like(mom_ref)
    scale = jnp.broadcast_to(ecols_ref[0:32, 0:1], (32, 128))
    shift = jnp.broadcast_to(ecols_ref[0:32, 1:2], (32, 128))
    constant = (iota((32, 128), 0) == 25) | (iota((32, 128), 0) == 26)
    shift = jnp.where(constant, 40.0, shift)

    def forward(q, carry):
        base = pl.multiple_of(q * 8, 8)
        firsts = []
        for r in range(8):
            t = jnp.tanh(scale * inv_ref[pl.ds(base + r, 1), :] + shift)
            s1_ref[base + r] = (1.0 - t * t).astype(BF16)
            firsts.append(t.astype(BF16))
        h1 = jnp.concatenate(firsts, axis=1)
        t2 = jnp.tanh(dot(w2_ref[...], h1))
        h2 = (jnp.concatenate([h1, h1], axis=0).astype(F32) + t2).astype(BF16)
        s2 = (1.0 - t2 * t2).astype(BF16)
        t3 = jnp.tanh(dot(w3_ref[...], h2))
        h3 = (jnp.concatenate([h2, h2], axis=0).astype(F32) + t3).astype(BF16)
        s3 = (1.0 - t3 * t3).astype(BF16)
        for r in range(8):
            part = slice(128 * r, 128 * r + 128)
            s2_ref[base + r] = s2[:, part]
            s3_ref[base + r] = s3[:, part]
            h3_ref[base + r] = h3[:, part]
        env = [[env_ref[c, pl.ds(base + r, 1), :] for r in range(8)] for c in range(4)]
        for n in range(8):
            rows = slice(16 * n, 16 * n + 16)
            tiles = [h3[rows, 128 * r : 128 * r + 128].astype(F32) for r in range(8)]
            for c in range(4):
                total = tiles[0] * env[c][0]
                for r in range(1, 8):
                    total = total + tiles[r] * env[c][r]
                mom_ref[c, rows] = mom_ref[c, rows] + total.astype(F32)
        return carry

    lax.fori_loop(0, ROWS // 8, forward, 0, unroll=True)

    low = iota((1, 128), 1) < 64
    nat_ref[:, 96:112, :] = jnp.zeros((4, 16, 128), F32)
    for c in range(4):
        m = mom_ref[c]
        m = (m + half_turn(m)) * (1.0 / K)
        for q in range(4):
            nat_ref[c, 25 * q : 25 * q + 25] = m[32 * q : 32 * q + 25]
        axis_ref[c] = jnp.where(low, m[0:8], m[8:16])
    for blk in range(7):
        mine = [nat_ref[c, 16 * blk : 16 * blk + 16] for c in range(4)]
        for p in range(8):
            total = mine[0] * axis_ref[0, p : p + 1]
            for c in range(1, 4):
                total = total + mine[c] * axis_ref[c, p : p + 1]
            feat_ref[128 * blk + 16 * p : 128 * blk + 16 * p + 16] = total.astype(BF16)

    both = dot(f1_ref[...], feat_ref[...])
    pre = jnp.where(low, both[0:240], both[240:480])
    t1 = jnp.tanh(pre + half_turn(pre) + cols_ref[0:240, 4:5])
    g1 = t1.astype(BF16)
    t2 = jnp.tanh(dot(f2_ref[0], g1) + cols_ref[0:240, 5:6])
    g2 = (g1.astype(F32) + t2).astype(BF16)
    t3 = jnp.tanh(dot(f3_ref[0], g2) + cols_ref[0:240, 6:7])
    d3 = jnp.broadcast_to(cols_ref[0:240, 7:8], (240, 128))
    back = dot(f3t_ref[...], (d3 * (1.0 - t3 * t3)).astype(BF16)).astype(BF16).astype(F32)
    d2 = (back + d3).astype(BF16).astype(F32)
    back = dot(f2t_ref[...], (d2 * (1.0 - t2 * t2)).astype(BF16)).astype(BF16).astype(F32)
    d1 = (back + d2).astype(BF16).astype(F32)
    d1 = d1 * (1.0 - t1 * t1)
    none = jnp.zeros((16, 128), F32)
    split = jnp.concatenate([jnp.where(low, d1, 0.0), none, jnp.where(low, 0.0, d1), none], axis=0)
    dfeat_ref[...] = dot(f1t_ref[...], split.astype(BF16)).astype(BF16).astype(F32)

    mom_ref[...] = jnp.zeros_like(mom_ref)
    for c in range(4):
        sums = [jnp.zeros((16, 128), F32)] * 8
        for blk in range(7):
            mine = nat_ref[c, 16 * blk : 16 * blk + 16]
            total = jnp.zeros((16, 128), F32)
            for p in range(8):
                d = dfeat_ref[128 * blk + 16 * p : 128 * blk + 16 * p + 16]
                total = total + d * axis_ref[c, p : p + 1]
                sums[p] = sums[p] + d * mine
            dnat_ref[c, 16 * blk : 16 * blk + 16] = total + half_turn(total)
        rows = jnp.concatenate([jnp.sum(s, axis=0, keepdims=True) for s in sums], axis=0)
        turned = half_turn(rows)
        dnat_ref[c, 0:8] = dnat_ref[c, 0:8] + jnp.where(low, rows, turned)
        dnat_ref[c, 8:16] = dnat_ref[c, 8:16] + jnp.where(low, turned, rows)
        for q in range(4):
            mom_ref[c, 32 * q : 32 * q + 25] = dnat_ref[c, 25 * q : 25 * q + 25] * (1.0 / K)

    def backward(q, carry):
        base = pl.multiple_of(q * 8, 8)
        outer, pushed = [], []
        for r in range(8):
            env = [env_ref[c, pl.ds(base + r, 1), :] for c in range(4)]
            parts = [None] * 4
            tiles = []
            for n in range(8):
                rows = slice(16 * n, 16 * n + 16)
                dm = [mom_ref[c, rows] for c in range(4)]
                tiles.append((dm[0] * env[0] + dm[1] * env[1] + dm[2] * env[2] + dm[3] * env[3]).astype(BF16))
                h = h3_ref[base + r, rows].astype(F32)
                parts = [dm[c] * h if s is None else s + dm[c] * h for c, s in enumerate(parts)]
            for c in range(4):
                denv_ref[c, pl.ds(base + r, 1), :] = jnp.sum(parts[c], axis=0, keepdims=True)
            d = jnp.concatenate(tiles, axis=0)
            outer.append(d)
            pushed.append(d * s3_ref[base + r])
        d3 = jnp.concatenate(outer, axis=1)
        back = dot(w3t_ref[...], jnp.concatenate(pushed, axis=1)).astype(BF16)
        d2 = back + d3[0:64] + d3[64:128]
        s2 = jnp.concatenate([s2_ref[base + r] for r in range(8)], axis=1)
        back = dot(w2t_ref[...], d2 * s2).astype(BF16)
        d1 = (back + d2[0:32] + d2[32:64]).astype(F32)
        for r in range(8):
            d = d1[:, 128 * r : 128 * r + 128] * s1_ref[base + r].astype(F32) * scale
            dinv_ref[pl.ds(base + r, 1), :] = jnp.sum(d, axis=0, keepdims=True)
        return carry

    lax.fori_loop(0, ROWS // 8, backward, 0, unroll=True)

    centre = [jnp.zeros((8, 128), F32)] * 3
    for q in range(ROWS // 8):
        at = slice(8 * q, 8 * q + 8)
        inverse = inv_ref[at]
        present = jnp.where(idx_ref[at] >= 0, 1.0, 0.0)
        offs = [off_ref[i, at] for i in range(3)]
        denv = [denv_ref[c, at] * present for c in range(4)]
        along = denv[1] * offs[0] + denv[2] * offs[1] + denv[3] * offs[2]
        square = inverse * inverse
        slope = (dinv_ref[at] + denv[0] + 2.0 * inverse * along) * (square * inverse) * -1.0
        for i in range(3):
            g = denv[i + 1] * square + slope * offs[i]
            grad_ref[i, at] = g
            centre[i] = centre[i] + g

    acc_ref[...] = jnp.zeros_like(acc_ref)
    which = iota((8, 128), 0)
    lead, next_up, rest = which % 3 == 0, which % 3 == 1, which >= 6
    spot = iota((16, 128), 0).astype(F32).astype(BF16)

    def scatter(q, carry):
        base = pl.multiple_of(q * 8, 8)
        left, right = [], []
        for r in range(8):
            at = pl.ds(base + r, 1)
            gx, gy, gz = (across(grad_ref[i, at, :], 8) for i in range(3))
            ox, oy, oz = (across(off_ref[i, at, :], 8) for i in range(3))
            g_even = jnp.where(lead, gx, jnp.where(next_up, gz, gy))
            o_even = jnp.where((which < 2) | rest, 1.0, jnp.where(which == 2, ox, jnp.where(which < 5, oy, oz)))
            g_odd = jnp.where(lead, gy, jnp.where(next_up, gx, gz))
            o_odd = jnp.where((which < 1) | rest, 1.0, jnp.where(which < 3, ox, jnp.where(which < 4, oy, oz)))
            halves = (-g_even * o_even, -g_odd * o_odd)
            term = jnp.concatenate([jnp.where(rest, t - t.astype(BF16).astype(F32), t) for t in halves], axis=0)
            term = term.astype(BF16)
            high = across(hi_ref[at, :], 16).astype(F32).astype(BF16)
            place = across(lo_ref[at, :], 16).astype(F32).astype(BF16)
            zero, one = jnp.zeros((16, 128), BF16), jnp.ones((16, 128), BF16)
            left.append(jnp.concatenate([jnp.where(high == float(h), term, zero) for h in range(14)], axis=0))
            right.append(
                jnp.concatenate([jnp.where(spot + float(16 * n) == place, one, zero) for n in range(8)], axis=0)
            )
        acc_ref[...] = acc_ref[...] + dot_last(jnp.concatenate(left, axis=1), jnp.concatenate(right, axis=1))
        return carry

    lax.fori_loop(0, ROWS // 8, scatter, 0, unroll=True)

    rows = [jnp.sum(s, axis=0, keepdims=True) for s in centre]
    rows = [s + half_turn(s) for s in rows]
    own = jnp.concatenate(
        [jnp.where(low, rows[0], rows[1]), jnp.where(low, rows[2], 0.0), jnp.zeros((6, 128), F32)], axis=0
    )
    mine = me & (RUN - 1)
    for a, b, c in OFFSETS:
        h, odd = divmod(slot_of(a, b, c), 2)
        even_terms = acc_ref[16 * h : 16 * h + 8]
        odd_terms = acc_ref[16 * h + 8 : 16 * h + 16]
        even_terms = even_terms + jnp.where(which < 2, pltpu.roll(even_terms, 2, axis=0), 0.0)
        odd_terms = odd_terms + jnp.where(which < 1, pltpu.roll(odd_terms, 2, axis=0), 0.0)
        if odd:
            tile = jnp.where(low, half_turn(even_terms), odd_terms)
        else:
            tile = jnp.where(low, even_terms, half_turn(odd_terms))
        if (a, b, c) == (0, 0, 0):
            tile = tile + own
        place = 8 * place_of(a, b, c)
        out_ref[(mine - (4 * b + c)) & (RUN - 1), place : place + 8, :] = tile


def regroup(recv_ref, out_ref, sum_ref):
    me = lax.axis_index("space")
    mine, run = me & (RUN - 1), me // RUN
    runs = out_ref.shape[0] // 4
    sum_ref[...] = jnp.zeros_like(sum_ref)
    for a, b, c in OFFSETS:
        moved = mine + 4 * b + c
        away = pl.multiple_of(8 * (SPAN - 2 * a - (moved >> 3)), 8)
        place = 8 * place_of(a, b, c)
        sum_ref[pl.ds(away, 8), :] = sum_ref[pl.ds(away, 8), :] + recv_ref[moved & (RUN - 1), place : place + 8, :]
    parts = [sum_ref[pl.ds(k, 8, stride=8), :] for k in range(6)]
    lane = iota((8, 128), 1) // 16
    for quarter in range(4):
        for side in range(2):
            total = jnp.zeros((8, 128), F32)
            for k in range(6):
                turn = (16 * k - 64 * side - 16 * quarter) % 128
                piece = parts[k] if turn == 0 else pltpu.roll(parts[k], turn, axis=1)
                total = jnp.where(lane == k, piece, total)
            for o in range(2 * SPAN + 1):
                target = quarter * runs + ((run + o - SPAN) & (runs - 1))
                out_ref[target, :, 128 * side : 128 * side + 128] = total[o : o + 1]


def finish(recv_ref, mean_ref, force_ref, virial_ref):
    run = lax.axis_index("space") // RUN
    runs = recv_ref.shape[0] // 4
    totals = []
    for m in range(4):
        total = recv_ref[m * runs + run]
        for o in range(-SPAN, SPAN + 1):
            if o != 0:
                total = total + recv_ref[m * runs + ((run - o) & (runs - 1))]
        totals.append(total)
    mean = (totals[0] + totals[1] + totals[2] + totals[3]) * 0.25
    spread = jnp.zeros_like(mean)
    for total in totals:
        spread = spread + (total - mean) * (total - mean)
    spread = spread * 0.25

    def component(x, k):
        half = x[:, 128 * (k % 2) : 128 * (k % 2) + 128]
        turn = (-16 * (k // 2)) % 128
        return half if turn == 0 else pltpu.roll(half, turn, axis=1)

    for k in range(3):
        mean_ref[k, 0] = component(mean, k)[:, 0:16]
    force = component(spread, 0)
    for k in range(1, 3):
        force = force + component(spread, k)
    force_ref[0] = force[:, 0:16]
    virial = component(spread, 3)
    for k in range(4, 12):
        virial = virial + component(spread, k)
    virial_ref[0] = virial[:, 0:16]


def call(body, out_shape, scratch=(), limit=16 << 20, **specs):
    return pl.pallas_call(
        body,
        out_shape=out_shape,
        scratch_shapes=list(scratch),
        compiler_params=pltpu.CompilerParams(vmem_limit_bytes=limit),
        **specs,
    )


def shaped(shape, dtype=F32):
    return jax.ShapeDtypeStruct(shape, dtype)


def local(
    positions, send_lists, neighbours,
    emb_scale, emb_shift, emb_middle, emb_mid_bias, emb_outer, emb_out_bias,
    fit_first, fit_first_bias, fit_second, fit_second_bias, fit_third, fit_third_bias, fit_readout,
):
    count = lax.axis_size("space")
    models = lax.axis_size("mp")
    runs = count // RUN
    packed = call(
        outgoing,
        shaped((count, 1, 384)),
        [
            pltpu.VMEM((6, 1, 128), I32),
            pltpu.VMEM(positions.shape, F32),
            pltpu.SemaphoreType.DMA((2,)),
        ],
        in_specs=[pl.BlockSpec(memory_space=pltpu.HBM)] * 2,
    )(jnp.transpose(send_lists, (1, 0, 2)), positions)
    arrived = lax.all_to_all(packed, "space", 0, 0)
    w2, w2t, w3, w3t, cols, ecols, f1, f1t, f2t, f3t = call(
        weights,
        (
            shaped((64, 32), BF16), shaped((32, 64), BF16), shaped((128, 64), BF16), shaped((64, 128), BF16),
            shaped((256, 128)), shaped((128, 128)), shaped((480, 896), BF16), shaped((896, 512), BF16),
            shaped((240, 240), BF16), shaped((240, 240), BF16),
        ),
        [pltpu.VMEM((128, 256), F32)],
    )(
        emb_scale, emb_shift, emb_middle, emb_mid_bias, emb_outer, emb_out_bias,
        fit_first, fit_first_bias, fit_second, fit_second_bias, fit_third, fit_third_bias, fit_readout,
    )
    pair = (ROWS, 128)
    terms = call(
        evaluate,
        shaped((RUN, 48, 128)),
        [
            pltpu.VMEM((12, 8, 128), I32), pltpu.VMEM((3, 8, 128), F32), pltpu.VMEM((8, 128), I32),
            pltpu.VMEM(pair, I32), pltpu.VMEM((3, *pair), F32), pltpu.VMEM(pair, F32), pltpu.VMEM((4, *pair), F32),
            pltpu.VMEM(pair, I32), pltpu.VMEM(pair, I32),
            pltpu.VMEM((ROWS, 32, 128), BF16), pltpu.VMEM((ROWS, 64, 128), BF16),
            pltpu.VMEM((ROWS, 128, 128), BF16), pltpu.VMEM((ROWS, 128, 128), BF16),
            pltpu.VMEM((4, 128, 128), F32), pltpu.VMEM((4, 112, 128), F32), pltpu.VMEM((4, 8, 128), F32),
            pltpu.VMEM((896, 128), BF16), pltpu.VMEM((896, 128), F32),
            pltpu.VMEM((4, 112, 128), F32),
            pltpu.VMEM((4, *pair), F32), pltpu.VMEM(pair, F32), pltpu.VMEM((3, *pair), F32),
            pltpu.VMEM((224, 128), F32),
        ],
        32 << 20,
    )(arrived, neighbours, w2, w2t, w3, w3t, cols, ecols, f1, f1t, fit_second, f2t, fit_third, f3t)
    near = [[RUN * u + v for v in range(RUN)] for u in range(runs)]
    terms = lax.all_to_all(terms, "space", 0, 0, axis_index_groups=near)
    terms = call(regroup, shaped((models * runs, 1, 256)), [pltpu.VMEM((64, 128), F32)])(terms)
    far = [[m * count + RUN * u + v for m in range(models) for u in range(runs)] for v in range(RUN)]
    terms = lax.all_to_all(terms, ("mp", "space"), 0, 0, axis_index_groups=far)
    quarter = positions.shape[1] // models
    return call(
        finish, (shaped((3, 1, 1, quarter)), shaped((1, 1, quarter)), shaped((1, 1, quarter)))
    )(terms)


def solution(mesh):
    params = [P("mp", None)] * 2 + [P("mp", None, None), P("mp", None)] * 5 + [P("mp", None)]
    return jax.shard_map(
        local,
        mesh=mesh,
        in_specs=(P(None, "space"), P("space", None, None), P(None, "space"), *params),
        out_specs=(P(None, "space", "mp", None), P("space", "mp", None), P("space", "mp", None)),
        check_vma=False,
    )
```

```python
import jax
import jax.numpy as jnp
from jax import lax
from jax.experimental import pallas as pl
from jax.experimental.pallas import tpu as pltpu
from jax.sharding import PartitionSpec as P

F32, BF16, I32 = jnp.float32, jnp.bfloat16, jnp.int32
K = 96
ROWS = K // 2
SOFTEN = 0.04
RUN = 8
SPAN = 3
OFFSETS = tuple((a, b, c) for a in (-1, 0, 1) for b in (-1, 0, 1) for c in (-1, 0, 1))


def slot_of(a, b, c):
    return (a + 1) * 9 + (b + 1) * 3 + (c + 1)


def step_of(a, b, c):
    return 16 * a + 4 * b + c


def place_of(a, b, c):
    return (3 if 4 * b + c <= -3 else 0) + a + 1


def iota(shape, dim):
    return lax.broadcasted_iota(I32, shape, dim)


def lanes_of(table, index):
    return jnp.take_along_axis(table, index, axis=1, mode="promise_in_bounds")


def across(row, count):
    return jnp.broadcast_to(row, (count, row.shape[1]))


def half_turn(x):
    return pltpu.roll(x, 64, axis=x.ndim - 1)


def dot(a, b):
    return jnp.dot(a, b, preferred_element_type=F32)


def dot_last(a, b):
    return lax.dot_general(a, b, (((1,), (1,)), ((), ())), preferred_element_type=F32)


def outgoing(lists_hbm, pos_hbm, out_ref, lists_ref, pos_ref, sems):
    fetches = [
        pltpu.make_async_copy(lists_hbm, lists_ref, sems.at[0]),
        pltpu.make_async_copy(pos_hbm, pos_ref, sems.at[1]),
    ]
    for fetch in fetches:
        fetch.start()
    for fetch in fetches:
        fetch.wait()
    count = out_ref.shape[0]
    me = lax.axis_index("space")
    lists = lists_ref[:, 0, :].astype(F32)
    pos = pos_ref[...]
    row_xy = jnp.concatenate([pos[0:1], pos[1:2]], axis=1)
    row_z = jnp.concatenate([pos[2:3], pos[2:3]], axis=1)
    for a, b, c in OFFSETS:
        target = lax.rem(me + step_of(a, b, c) + count, count)
        block = next((2 * s + (0 if v > 0 else 1) for s, v in enumerate((a, b, c)) if v), None)
        first = jnp.zeros((1, 128), F32) if block is None else lists[block : block + 1]
        out_ref[target, :, 0:128] = first
        out_ref[target, :, 128:256] = row_xy
        out_ref[target, :, 256:384] = row_z


def grouped(rows, cols, by_row):
    r, c = iota((rows, cols), 0), iota((rows, cols), 1)
    wide, narrow = (r, c) if by_row else (c, r)
    hit = (narrow == (wide // 32) * 25 + wide % 32) & (wide % 32 < 25)
    return hit.astype(F32).astype(BF16)


def eye(n):
    return (iota((n, n), 0) == iota((n, n), 1)).astype(F32).astype(BF16)


def weights(
    scale_ref, shift_ref, mid_ref, mid_b_ref, outer_ref, outer_b_ref,
    one_ref, one_b_ref, two_ref, two_b_ref, three_ref, three_b_ref, read_ref,
    w2_ref, w2t_ref, w3_ref, w3t_ref, cols_ref, ecols_ref, f1_ref, f1t_ref, f2t_ref, f3t_ref,
    stack_ref,
):
    w2 = dot(dot(grouped(64, 50, True), mid_ref[0]).astype(BF16), grouped(25, 32, False)).astype(BF16)
    w3 = dot(dot(grouped(128, 100, True), outer_ref[0]).astype(BF16), grouped(50, 64, False)).astype(BF16)
    w2t_ref[...] = dot_last(eye(32), w2).astype(BF16)
    w3t_ref[...] = dot_last(eye(64), w3).astype(BF16)
    f2t_ref[...] = dot_last(eye(240), two_ref[0]).astype(BF16)
    f3t_ref[...] = dot_last(eye(240), three_ref[0]).astype(BF16)
    stack_ref[...] = jnp.zeros_like(stack_ref)
    small = (scale_ref, shift_ref, mid_b_ref, outer_b_ref, one_b_ref, two_b_ref, three_b_ref, read_ref)
    for i, ref in enumerate(small):
        stack_ref[i : i + 1, 0 : ref.shape[1]] = ref[...].astype(F32)
    turned = jnp.transpose(stack_ref[...], (1, 0))
    cols_ref[...] = turned
    ecols_ref[...] = jnp.zeros_like(ecols_ref)
    for q in range(4):
        ecols_ref[32 * q : 32 * q + 25, :] = turned[25 * q : 25 * q + 25]
    for w, ref, column in ((w2, w2_ref, 2), (w3, w3_ref, 3)):
        bias = jnp.broadcast_to(ecols_ref[0 : w.shape[0], column : column + 1], w.shape)
        whole = bias.astype(BF16).astype(F32)
        lane = iota(w.shape, 1)
        ref[...] = jnp.where(lane == 25, whole, jnp.where(lane == 26, bias - whole, w.astype(F32))).astype(BF16)
    f1t_ref[...] = jnp.zeros_like(f1t_ref)
    for part in range(2):
        r, c = iota((256, 128), 0), iota((256, 128), 1)
        pick = (r == (c % 16) * 16 + c // 16 + 8 * part).astype(F32).astype(BF16)
        r, c = iota((128, 256), 0), iota((128, 256), 1)
        pick_t = (c == (r % 16) * 16 + r // 16 + 8 * part).astype(F32).astype(BF16)
        for blk in range(7):
            wide = min(256, 1600 - 256 * blk)
            piece = one_ref[0, :, 256 * blk : 256 * blk + wide]
            f1_ref[240 * part : 240 * part + 240, 128 * blk : 128 * blk + 128] = dot(
                piece, pick[0:wide]
            ).astype(BF16)
            f1t_ref[128 * blk : 128 * blk + 128, 256 * part : 256 * part + 240] = dot_last(
                pick_t[:, 0:wide], piece
            ).astype(BF16)


def resolve(me, count, recv_ref, num_ref, ext_ref, code_ref):
    def source(a, b, c):
        return lax.rem(me - step_of(a, b, c) + count, count)

    def listed(a, b, c):
        return recv_ref[source(a, b, c), :, 0:128].astype(I32)

    def coded(a, b, c):
        return listed(a, b, c) + 64 * slot_of(a, b, c)

    num_ref[...] = jnp.zeros_like(num_ref)
    pairs = [(b, c) for b in (1, -1) for c in (-1, 0, 1)]
    for i, (b, c) in enumerate(pairs):
        entry = listed(0, b, c)
        num_ref[0, i : i + 1] = entry
        num_ref[1, i : i + 1] = entry + 64 * slot_of(0, b, c)
        num_ref[2, i : i + 1] = coded(1, b, c)
        num_ref[3, i : i + 1] = coded(-1, b, c)
    entry = num_ref[0]
    index = (entry + 64) & 127
    middle = jnp.where(
        entry < 64,
        num_ref[1],
        jnp.where(entry < 192, lanes_of(num_ref[2], index), lanes_of(num_ref[3], index)),
    )
    num_ref[4] = middle
    for i, c in enumerate((1, -1)):
        entry = listed(0, 0, c)
        num_ref[5, i : i + 1] = entry
        num_ref[6, i : i + 1] = entry + 64 * slot_of(0, 0, c)
        num_ref[7, i : i + 1] = coded(1, 0, c)
        num_ref[8, i : i + 1] = coded(-1, 0, c)
        num_ref[9, i : i + 1] = num_ref[4, c + 1 : c + 2]
        num_ref[10, i : i + 1] = num_ref[4, c + 4 : c + 5]
    entry = num_ref[5]
    index = (entry + 64) & 127
    found = num_ref[6]
    for i, least in enumerate((64, 192, 320, 448)):
        found = jnp.where(entry < least, found, lanes_of(num_ref[7 + i], index))
    num_ref[11] = found
    code_ref[0:1] = 64 * slot_of(0, 0, 0) + (iota((1, 128), 1) & 63)
    code_ref[1:2] = coded(1, 0, 0)
    code_ref[2:3] = coded(-1, 0, 0)
    code_ref[3:4] = num_ref[4, 1:2]
    code_ref[4:5] = num_ref[4, 4:5]
    code_ref[5:7] = num_ref[11, 0:2]
    code_ref[7:8] = jnp.zeros((1, 128), I32)
    code = code_ref[...]
    atom = code & 63
    owner = code >> 6
    spots = [jnp.zeros((8, 128), F32)] * 3
    for a, b, c in OFFSETS:
        e = source(a, b, c)
        row_xy = across(recv_ref[e, :, 128:256], 8)
        row_z = across(recv_ref[e, :, 256:384], 8)
        here = owner == slot_of(a, b, c)
        got = (lanes_of(row_xy, atom), lanes_of(row_xy, atom + 64), lanes_of(row_z, atom))
        spots = [jnp.where(here, g - float(o), s) for g, o, s in zip(got, (a, b, c), spots)]
    for i in range(3):
        ext_ref[i] = spots[i]


def evaluate(
    recv_ref, nb_ref, w2_ref, w2t_ref, w3_ref, w3t_ref, cols_ref, ecols_ref,
    f1_ref, f1t_ref, f2_ref, f2t_ref, f3_ref, f3t_ref,
    out_ref,
    num_ref, ext_ref, code_ref, idx_ref, off_ref, inv_ref, env_ref, hi_ref, lo_ref,
    s1_ref, s2_ref, s3_ref, h3_ref, mom_ref, nat_ref, axis_ref, feat_ref, dfeat_ref,
    dnat_ref, denv_ref, dinv_ref, grad_ref, acc_ref,
):
    count = recv_ref.shape[0]
    me = lax.axis_index("space")
    resolve(me, count, recv_ref, num_ref, ext_ref, code_ref)

    idx_ref[:, 0:64] = nb_ref[0:ROWS, :]
    idx_ref[:, 64:128] = nb_ref[ROWS:K, :]
    for q in range(ROWS // 8):
        at = slice(8 * q, 8 * q + 8)
        ids = idx_ref[at]
        present = jnp.where(ids >= 0, 1.0, 0.0)
        row, lane = (ids + 64) >> 7, (ids + 64) & 127
        spots = [jnp.zeros((8, 128), F32)] * 3
        code = jnp.zeros((8, 128), I32)
        for k in range(7):
            here = row == k
            spots = [
                jnp.where(here, lanes_of(across(ext_ref[i, k : k + 1], 8), lane), s)
                for i, s in enumerate(spots)
            ]
            code = jnp.where(here, lanes_of(across(code_ref[k : k + 1], 8), lane), code)
        offs = [s - ext_ref[i, 0:1] for i, s in enumerate(spots)]
        inverse = lax.rsqrt(offs[0] * offs[0] + offs[1] * offs[1] + offs[2] * offs[2] + SOFTEN)
        inv_ref[at] = inverse
        env_ref[0, at] = inverse * present
        for i in range(3):
            off_ref[i, at] = offs[i]
            env_ref[i + 1, at] = (inverse * inverse) * offs[i] * present
        hi_ref[at] = jnp.where(ids >= 0, code >> 7, -1)
        lo_ref[at] = code & 127

    mom_ref[...] = jnp.zeros_like(mom_ref)
    scale = jnp.broadcast_to(ecols_ref[0:32, 0:1], (32, 128))
    shift = jnp.broadcast_to(ecols_ref[0:32, 1:2], (32, 128))
    constant = (iota((32, 128), 0) == 25) | (iota((32, 128), 0) == 26)
    shift = jnp.where(constant, 40.0, shift)

    def forward(q, carry):
        base = pl.multiple_of(q * 8, 8)
        firsts = []
        for r in range(8):
            t = jnp.tanh(scale * inv_ref[pl.ds(base + r, 1), :] + shift)
            s1_ref[base + r] = (1.0 - t * t).astype(BF16)
            firsts.append(t.astype(BF16))
        h1 = jnp.concatenate(firsts, axis=1)
        t2 = jnp.tanh(dot(w2_ref[...], h1))
        h2 = (jnp.concatenate([h1, h1], axis=0).astype(F32) + t2).astype(BF16)
        s2 = (1.0 - t2 * t2).astype(BF16)
        t3 = jnp.tanh(dot(w3_ref[...], h2))
        h3 = (jnp.concatenate([h2, h2], axis=0).astype(F32) + t3).astype(BF16)
        s3 = (1.0 - t3 * t3).astype(BF16)
        for r in range(8):
            part = slice(128 * r, 128 * r + 128)
            s2_ref[base + r] = s2[:, part]
            s3_ref[base + r] = s3[:, part]
            h3_ref[base + r] = h3[:, part]
        env = [[env_ref[c, pl.ds(base + r, 1), :] for r in range(8)] for c in range(4)]
        for n in range(8):
            rows = slice(16 * n, 16 * n + 16)
            tiles = [h3[rows, 128 * r : 128 * r + 128].astype(F32) for r in range(8)]
            for c in range(4):
                total = tiles[0] * env[c][0]
                for r in range(1, 8):
                    total = total + tiles[r] * env[c][r]
                mom_ref[c, rows] = mom_ref[c, rows] + total.astype(F32)
        return carry

    lax.fori_loop(0, ROWS // 8, forward, 0, unroll=True)

    low = iota((1, 128), 1) < 64
    nat_ref[:, 96:112, :] = jnp.zeros((4, 16, 128), F32)
    for c in range(4):
        m = mom_ref[c]
        m = (m + half_turn(m)) * (1.0 / K)
        for q in range(4):
            nat_ref[c, 25 * q : 25 * q + 25] = m[32 * q : 32 * q + 25]
        axis_ref[c] = jnp.where(low, m[0:8], m[8:16])
    for blk in range(7):
        mine = [nat_ref[c, 16 * blk : 16 * blk + 16] for c in range(4)]
        for p in range(8):
            total = mine[0] * axis_ref[0, p : p + 1]
            for c in range(1, 4):
                total = total + mine[c] * axis_ref[c, p : p + 1]
            feat_ref[128 * blk + 16 * p : 128 * blk + 16 * p + 16] = total.astype(BF16)

    both = dot(f1_ref[...], feat_ref[...])
    pre = jnp.where(low, both[0:240], both[240:480])
    t1 = jnp.tanh(pre + half_turn(pre) + cols_ref[0:240, 4:5])
    g1 = t1.astype(BF16)
    t2 = jnp.tanh(dot(f2_ref[0], g1) + cols_ref[0:240, 5:6])
    g2 = (g1.astype(F32) + t2).astype(BF16)
    t3 = jnp.tanh(dot(f3_ref[0], g2) + cols_ref[0:240, 6:7])
    d3 = jnp.broadcast_to(cols_ref[0:240, 7:8], (240, 128))
    back = dot(f3t_ref[...], (d3 * (1.0 - t3 * t3)).astype(BF16)).astype(BF16).astype(F32)
    d2 = (back + d3).astype(BF16).astype(F32)
    back = dot(f2t_ref[...], (d2 * (1.0 - t2 * t2)).astype(BF16)).astype(BF16).astype(F32)
    d1 = (back + d2).astype(BF16).astype(F32)
    d1 = d1 * (1.0 - t1 * t1)
    none = jnp.zeros((16, 128), F32)
    split = jnp.concatenate([jnp.where(low, d1, 0.0), none, jnp.where(low, 0.0, d1), none], axis=0)
    dfeat_ref[...] = dot(f1t_ref[...], split.astype(BF16)).astype(BF16).astype(F32)

    mom_ref[...] = jnp.zeros_like(mom_ref)
    for c in range(4):
        sums = [jnp.zeros((16, 128), F32)] * 8
        for blk in range(7):
            mine = nat_ref[c, 16 * blk : 16 * blk + 16]
            total = jnp.zeros((16, 128), F32)
            for p in range(8):
                d = dfeat_ref[128 * blk + 16 * p : 128 * blk + 16 * p + 16]
                total = total + d * axis_ref[c, p : p + 1]
                sums[p] = sums[p] + d * mine
            dnat_ref[c, 16 * blk : 16 * blk + 16] = total + half_turn(total)
        rows = jnp.concatenate([jnp.sum(s, axis=0, keepdims=True) for s in sums], axis=0)
        turned = half_turn(rows)
        dnat_ref[c, 0:8] = dnat_ref[c, 0:8] + jnp.where(low, rows, turned)
        dnat_ref[c, 8:16] = dnat_ref[c, 8:16] + jnp.where(low, turned, rows)
        for q in range(4):
            mom_ref[c, 32 * q : 32 * q + 25] = dnat_ref[c, 25 * q : 25 * q + 25] * (1.0 / K)

    def backward(q, carry):
        base = pl.multiple_of(q * 4, 4)
        outer, pushed = [], []
        for r in range(4):
            env = [env_ref[c, pl.ds(base + r, 1), :] for c in range(4)]
            parts = [None] * 4
            tiles = []
            for n in range(8):
                rows = slice(16 * n, 16 * n + 16)
                dm = [mom_ref[c, rows] for c in range(4)]
                tiles.append((dm[0] * env[0] + dm[1] * env[1] + dm[2] * env[2] + dm[3] * env[3]).astype(BF16))
                h = h3_ref[base + r, rows].astype(F32)
                parts = [dm[c] * h if s is None else s + dm[c] * h for c, s in enumerate(parts)]
            for c in range(4):
                denv_ref[c, pl.ds(base + r, 1), :] = jnp.sum(parts[c], axis=0, keepdims=True)
            d = jnp.concatenate(tiles, axis=0)
            outer.append(d)
            pushed.append(d * s3_ref[base + r])
        d3 = jnp.concatenate(outer, axis=1)
        back = dot(w3t_ref[...], jnp.concatenate(pushed, axis=1)).astype(BF16)
        d2 = back + d3[0:64] + d3[64:128]
        s2 = jnp.concatenate([s2_ref[base + r] for r in range(4)], axis=1)
        back = dot(w2t_ref[...], d2 * s2).astype(BF16)
        d1 = (back + d2[0:32] + d2[32:64]).astype(F32)
        for r in range(4):
            d = d1[:, 128 * r : 128 * r + 128] * s1_ref[base + r].astype(F32) * scale
            dinv_ref[pl.ds(base + r, 1), :] = jnp.sum(d, axis=0, keepdims=True)
        return carry

    lax.fori_loop(0, ROWS // 4, backward, 0, unroll=True)

    centre = [jnp.zeros((8, 128), F32)] * 3
    for q in range(ROWS // 8):
        at = slice(8 * q, 8 * q + 8)
        inverse = inv_ref[at]
        present = jnp.where(idx_ref[at] >= 0, 1.0, 0.0)
        offs = [off_ref[i, at] for i in range(3)]
        denv = [denv_ref[c, at] * present for c in range(4)]
        along = denv[1] * offs[0] + denv[2] * offs[1] + denv[3] * offs[2]
        square = inverse * inverse
        slope = (dinv_ref[at] + denv[0] + 2.0 * inverse * along) * (square * inverse) * -1.0
        for i in range(3):
            g = denv[i + 1] * square + slope * offs[i]
            grad_ref[i, at] = g
            centre[i] = centre[i] + g

    acc_ref[...] = jnp.zeros_like(acc_ref)
    which = iota((8, 128), 0)
    lead, next_up, rest = which % 3 == 0, which % 3 == 1, which >= 6
    spot = iota((16, 128), 0).astype(F32).astype(BF16)

    def scatter(q, carry):
        base = pl.multiple_of(q * 8, 8)
        left, right = [], []
        for r in range(8):
            at = pl.ds(base + r, 1)
            gx, gy, gz = (across(grad_ref[i, at, :], 8) for i in range(3))
            ox, oy, oz = (across(off_ref[i, at, :], 8) for i in range(3))
            g_even = jnp.where(lead, gx, jnp.where(next_up, gz, gy))
            o_even = jnp.where((which < 2) | rest, 1.0, jnp.where(which == 2, ox, jnp.where(which < 5, oy, oz)))
            g_odd = jnp.where(lead, gy, jnp.where(next_up, gx, gz))
            o_odd = jnp.where((which < 1) | rest, 1.0, jnp.where(which < 3, ox, jnp.where(which < 4, oy, oz)))
            halves = (-g_even * o_even, -g_odd * o_odd)
            term = jnp.concatenate([jnp.where(rest, t - t.astype(BF16).astype(F32), t) for t in halves], axis=0)
            term = term.astype(BF16)
            high = across(hi_ref[at, :], 16).astype(F32).astype(BF16)
            place = across(lo_ref[at, :], 16).astype(F32).astype(BF16)
            zero, one = jnp.zeros((16, 128), BF16), jnp.ones((16, 128), BF16)
            left.append(jnp.concatenate([jnp.where(high == float(h), term, zero) for h in range(14)], axis=0))
            right.append(
                jnp.concatenate([jnp.where(spot + float(16 * n) == place, one, zero) for n in range(8)], axis=0)
            )
        acc_ref[...] = acc_ref[...] + dot_last(jnp.concatenate(left, axis=1), jnp.concatenate(right, axis=1))
        return carry

    lax.fori_loop(0, ROWS // 8, scatter, 0, unroll=True)

    rows = [jnp.sum(s, axis=0, keepdims=True) for s in centre]
    rows = [s + half_turn(s) for s in rows]
    own = jnp.concatenate(
        [jnp.where(low, rows[0], rows[1]), jnp.where(low, rows[2], 0.0), jnp.zeros((6, 128), F32)], axis=0
    )
    mine = me & (RUN - 1)
    for a, b, c in OFFSETS:
        h, odd = divmod(slot_of(a, b, c), 2)
        even_terms = acc_ref[16 * h : 16 * h + 8]
        odd_terms = acc_ref[16 * h + 8 : 16 * h + 16]
        even_terms = even_terms + jnp.where(which < 2, pltpu.roll(even_terms, 2, axis=0), 0.0)
        odd_terms = odd_terms + jnp.where(which < 1, pltpu.roll(odd_terms, 2, axis=0), 0.0)
        if odd:
            tile = jnp.where(low, half_turn(even_terms), odd_terms)
        else:
            tile = jnp.where(low, even_terms, half_turn(odd_terms))
        if (a, b, c) == (0, 0, 0):
            tile = tile + own
        place = 6 * place_of(a, b, c)
        out_ref[(mine - (4 * b + c)) & (RUN - 1), place : place + 6, :] = tile[0:6]


def regroup(recv_ref, out_ref, sum_ref):
    me = lax.axis_index("space")
    mine, run = me & (RUN - 1), me // RUN
    runs = out_ref.shape[0] // 4
    sum_ref[...] = jnp.zeros_like(sum_ref)
    for a, b, c in OFFSETS:
        moved = mine + 4 * b + c
        away = pl.multiple_of(8 * (SPAN - 2 * a - (moved >> 3)), 8)
        place = 6 * place_of(a, b, c)
        sum_ref[pl.ds(away, 6), :] = sum_ref[pl.ds(away, 6), :] + recv_ref[moved & (RUN - 1), place : place + 6, :]
    parts = [sum_ref[pl.ds(k, 8, stride=8), :] for k in range(6)]
    lane = iota((8, 128), 1) // 16
    for quarter in range(4):
        for side in range(2):
            total = jnp.zeros((8, 128), F32)
            for k in range(6):
                turn = (16 * k - 64 * side - 16 * quarter) % 128
                piece = parts[k] if turn == 0 else pltpu.roll(parts[k], turn, axis=1)
                total = jnp.where(lane == k, piece, total)
            for o in range(2 * SPAN + 1):
                target = quarter * runs + ((run + o - SPAN) & (runs - 1))
                out_ref[target, :, 128 * side : 128 * side + 128] = total[o : o + 1]


def finish(recv_ref, mean_ref, force_ref, virial_ref):
    run = lax.axis_index("space") // RUN
    runs = recv_ref.shape[0] // 4
    totals = []
    for m in range(4):
        total = recv_ref[m * runs + run]
        for o in range(-SPAN, SPAN + 1):
            if o != 0:
                total = total + recv_ref[m * runs + ((run - o) & (runs - 1))]
        totals.append(total)
    mean = (totals[0] + totals[1] + totals[2] + totals[3]) * 0.25
    spread = jnp.zeros_like(mean)
    for total in totals:
        spread = spread + (total - mean) * (total - mean)
    spread = spread * 0.25

    def component(x, k):
        half = x[:, 128 * (k % 2) : 128 * (k % 2) + 128]
        turn = (-16 * (k // 2)) % 128
        return half if turn == 0 else pltpu.roll(half, turn, axis=1)

    for k in range(3):
        mean_ref[k, 0] = component(mean, k)[:, 0:16]
    force = component(spread, 0)
    for k in range(1, 3):
        force = force + component(spread, k)
    force_ref[0] = force[:, 0:16]
    virial = component(spread, 3)
    for k in range(4, 12):
        virial = virial + component(spread, k)
    virial_ref[0] = virial[:, 0:16]


def call(body, out_shape, scratch=(), limit=16 << 20, **specs):
    return pl.pallas_call(
        body,
        out_shape=out_shape,
        scratch_shapes=list(scratch),
        compiler_params=pltpu.CompilerParams(vmem_limit_bytes=limit),
        **specs,
    )


def shaped(shape, dtype=F32):
    return jax.ShapeDtypeStruct(shape, dtype)


def local(
    positions, send_lists, neighbours,
    emb_scale, emb_shift, emb_middle, emb_mid_bias, emb_outer, emb_out_bias,
    fit_first, fit_first_bias, fit_second, fit_second_bias, fit_third, fit_third_bias, fit_readout,
):
    count = lax.axis_size("space")
    models = lax.axis_size("mp")
    runs = count // RUN
    packed = call(
        outgoing,
        shaped((count, 1, 384)),
        [
            pltpu.VMEM((6, 1, 128), I32),
            pltpu.VMEM(positions.shape, F32),
            pltpu.SemaphoreType.DMA((2,)),
        ],
        63 << 20,
        in_specs=[pl.BlockSpec(memory_space=pl.ANY)] * 2,
    )(jnp.transpose(send_lists, (1, 0, 2)), positions)
    arrived = lax.all_to_all(packed, "space", 0, 0)
    w2, w2t, w3, w3t, cols, ecols, f1, f1t, f2t, f3t = call(
        weights,
        (
            shaped((64, 32), BF16), shaped((32, 64), BF16), shaped((128, 64), BF16), shaped((64, 128), BF16),
            shaped((256, 128)), shaped((128, 128)), shaped((480, 896), BF16), shaped((896, 512), BF16),
            shaped((240, 240), BF16), shaped((240, 240), BF16),
        ),
        [pltpu.VMEM((128, 256), F32)],
    )(
        emb_scale, emb_shift, emb_middle, emb_mid_bias, emb_outer, emb_out_bias,
        fit_first, fit_first_bias, fit_second, fit_second_bias, fit_third, fit_third_bias, fit_readout,
    )
    pair = (ROWS, 128)
    terms = call(
        evaluate,
        shaped((RUN, 36, 128)),
        [
            pltpu.VMEM((12, 8, 128), I32), pltpu.VMEM((3, 8, 128), F32), pltpu.VMEM((8, 128), I32),
            pltpu.VMEM(pair, I32), pltpu.VMEM((3, *pair), F32), pltpu.VMEM(pair, F32), pltpu.VMEM((4, *pair), F32),
            pltpu.VMEM(pair, I32), pltpu.VMEM(pair, I32),
            pltpu.VMEM((ROWS, 32, 128), BF16), pltpu.VMEM((ROWS, 64, 128), BF16),
            pltpu.VMEM((ROWS, 128, 128), BF16), pltpu.VMEM((ROWS, 128, 128), BF16),
            pltpu.VMEM((4, 128, 128), F32), pltpu.VMEM((4, 112, 128), F32), pltpu.VMEM((4, 8, 128), F32),
            pltpu.VMEM((896, 128), BF16), pltpu.VMEM((896, 128), F32),
            pltpu.VMEM((4, 112, 128), F32),
            pltpu.VMEM((4, *pair), F32), pltpu.VMEM(pair, F32), pltpu.VMEM((3, *pair), F32),
            pltpu.VMEM((224, 128), F32),
        ],
        32 << 20,
    )(arrived, neighbours, w2, w2t, w3, w3t, cols, ecols, f1, f1t, fit_second, f2t, fit_third, f3t)
    near = [[RUN * u + v for v in range(RUN)] for u in range(runs)]
    terms = lax.all_to_all(terms, "space", 0, 0, axis_index_groups=near)
    terms = call(regroup, shaped((models * runs, 1, 256)), [pltpu.VMEM((64, 128), F32)])(terms)
    far = [[m * count + RUN * u + v for m in range(models) for u in range(runs)] for v in range(RUN)]
    terms = lax.all_to_all(terms, ("mp", "space"), 0, 0, axis_index_groups=far)
    quarter = positions.shape[1] // models
    return call(
        finish, (shaped((3, 1, 1, quarter)), shaped((1, 1, quarter)), shaped((1, 1, quarter)))
    )(terms)


def solution(mesh):
    params = [P("mp", None)] * 2 + [P("mp", None, None), P("mp", None)] * 5 + [P("mp", None)]
    return jax.shard_map(
        local,
        mesh=mesh,
        in_specs=(P(None, "space"), P("space", None, None), P(None, "space"), *params),
        out_specs=(P(None, "space", "mp", None), P("space", "mp", None), P("space", "mp", None)),
        check_vma=False,
    )
```

```python
import jax
import jax.numpy as jnp
from jax import lax
from jax.experimental import pallas as pl
from jax.experimental.pallas import tpu as pltpu
from jax.sharding import PartitionSpec as P

F32, BF16, I32 = jnp.float32, jnp.bfloat16, jnp.int32
K = 96
ROWS = K // 2
SOFTEN = 0.04
RUN = 8
SPAN = 3
OFFSETS = tuple((a, b, c) for a in (-1, 0, 1) for b in (-1, 0, 1) for c in (-1, 0, 1))


def slot_of(a, b, c):
    return (a + 1) * 9 + (b + 1) * 3 + (c + 1)


def step_of(a, b, c):
    return 16 * a + 4 * b + c


def place_of(a, b, c):
    return (3 if 4 * b + c <= -3 else 0) + a + 1


def iota(shape, dim):
    return lax.broadcasted_iota(I32, shape, dim)


def lanes_of(table, index):
    return jnp.take_along_axis(table, index, axis=1, mode="promise_in_bounds")


def across(row, count):
    return jnp.broadcast_to(row, (count, row.shape[1]))


def half_turn(x):
    return pltpu.roll(x, 64, axis=x.ndim - 1)


def dot(a, b):
    return jnp.dot(a, b, preferred_element_type=F32)


def dot_last(a, b):
    return lax.dot_general(a, b, (((1,), (1,)), ((), ())), preferred_element_type=F32)


def outgoing(lists_hbm, pos_hbm, out_ref, lists_ref, pos_ref, sems):
    fetches = [
        pltpu.make_async_copy(lists_hbm, lists_ref, sems.at[0]),
        pltpu.make_async_copy(pos_hbm, pos_ref, sems.at[1]),
    ]
    for fetch in fetches:
        fetch.start()
    for fetch in fetches:
        fetch.wait()
    count = out_ref.shape[0]
    me = lax.axis_index("space")
    lists = lists_ref[:, 0, :].astype(F32)
    pos = pos_ref[...]
    row_xy = jnp.concatenate([pos[0:1], pos[1:2]], axis=1)
    row_z = pos[2:3]
    for a, b, c in OFFSETS:
        target = lax.rem(me + step_of(a, b, c) + count, count)
        block = next((2 * s + (0 if v > 0 else 1) for s, v in enumerate((a, b, c)) if v), None)
        first = jnp.zeros((1, 128), F32) if block is None else lists[block : block + 1]
        out_ref[target, :, 0:128] = first
        out_ref[target, :, 128:256] = row_xy
        out_ref[target, :, 256:320] = row_z


def grouped(rows, cols, by_row):
    r, c = iota((rows, cols), 0), iota((rows, cols), 1)
    wide, narrow = (r, c) if by_row else (c, r)
    hit = (narrow == (wide // 32) * 25 + wide % 32) & (wide % 32 < 25)
    return hit.astype(F32).astype(BF16)


def eye(n):
    return (iota((n, n), 0) == iota((n, n), 1)).astype(F32).astype(BF16)


def weights(
    scale_ref, shift_ref, mid_ref, mid_b_ref, outer_ref, outer_b_ref,
    one_ref, one_b_ref, two_ref, two_b_ref, three_ref, three_b_ref, read_ref,
    w2_ref, w2t_ref, w3_ref, w3t_ref, cols_ref, ecols_ref, f1_ref, f1t_ref, f2t_ref, f3t_ref,
    stack_ref,
):
    w2 = dot(dot(grouped(64, 50, True), mid_ref[0]).astype(BF16), grouped(25, 32, False)).astype(BF16)
    w3 = dot(dot(grouped(128, 100, True), outer_ref[0]).astype(BF16), grouped(50, 64, False)).astype(BF16)
    w2t_ref[...] = dot_last(eye(32), w2).astype(BF16)
    w3t_ref[...] = dot_last(eye(64), w3).astype(BF16)
    f2t_ref[...] = dot_last(eye(240), two_ref[0]).astype(BF16)
    f3t_ref[...] = dot_last(eye(240), three_ref[0]).astype(BF16)
    stack_ref[...] = jnp.zeros_like(stack_ref)
    small = (scale_ref, shift_ref, mid_b_ref, outer_b_ref, one_b_ref, two_b_ref, three_b_ref, read_ref)
    for i, ref in enumerate(small):
        stack_ref[i : i + 1, 0 : ref.shape[1]] = ref[...].astype(F32)
    turned = jnp.transpose(stack_ref[...], (1, 0))
    cols_ref[...] = turned
    ecols_ref[...] = jnp.zeros_like(ecols_ref)
    for q in range(4):
        ecols_ref[32 * q : 32 * q + 25, :] = turned[25 * q : 25 * q + 25]
    for w, ref, column in ((w2, w2_ref, 2), (w3, w3_ref, 3)):
        bias = jnp.broadcast_to(ecols_ref[0 : w.shape[0], column : column + 1], w.shape)
        whole = bias.astype(BF16).astype(F32)
        lane = iota(w.shape, 1)
        ref[...] = jnp.where(lane == 25, whole, jnp.where(lane == 26, bias - whole, w.astype(F32))).astype(BF16)
    f1t_ref[...] = jnp.zeros_like(f1t_ref)
    for part in range(2):
        r, c = iota((256, 128), 0), iota((256, 128), 1)
        pick = (r == (c % 16) * 16 + c // 16 + 8 * part).astype(F32).astype(BF16)
        r, c = iota((128, 256), 0), iota((128, 256), 1)
        pick_t = (c == (r % 16) * 16 + r // 16 + 8 * part).astype(F32).astype(BF16)
        for blk in range(7):
            wide = min(256, 1600 - 256 * blk)
            piece = one_ref[0, :, 256 * blk : 256 * blk + wide]
            f1_ref[240 * part : 240 * part + 240, 128 * blk : 128 * blk + 128] = dot(
                piece, pick[0:wide]
            ).astype(BF16)
            f1t_ref[128 * blk : 128 * blk + 128, 256 * part : 256 * part + 240] = dot_last(
                pick_t[:, 0:wide], piece
            ).astype(BF16)


def resolve(me, count, recv_ref, num_ref, ext_ref, code_ref):
    def source(a, b, c):
        return lax.rem(me - step_of(a, b, c) + count, count)

    def listed(a, b, c):
        return recv_ref[source(a, b, c), :, 0:128].astype(I32)

    def coded(a, b, c):
        return listed(a, b, c) + 64 * slot_of(a, b, c)

    num_ref[...] = jnp.zeros_like(num_ref)
    pairs = [(b, c) for b in (1, -1) for c in (-1, 0, 1)]
    for i, (b, c) in enumerate(pairs):
        entry = listed(0, b, c)
        num_ref[0, i : i + 1] = entry
        num_ref[1, i : i + 1] = entry + 64 * slot_of(0, b, c)
        num_ref[2, i : i + 1] = coded(1, b, c)
        num_ref[3, i : i + 1] = coded(-1, b, c)
    entry = num_ref[0]
    index = (entry + 64) & 127
    middle = jnp.where(
        entry < 64,
        num_ref[1],
        jnp.where(entry < 192, lanes_of(num_ref[2], index), lanes_of(num_ref[3], index)),
    )
    num_ref[4] = middle
    for i, c in enumerate((1, -1)):
        entry = listed(0, 0, c)
        num_ref[5, i : i + 1] = entry
        num_ref[6, i : i + 1] = entry + 64 * slot_of(0, 0, c)
        num_ref[7, i : i + 1] = coded(1, 0, c)
        num_ref[8, i : i + 1] = coded(-1, 0, c)
        num_ref[9, i : i + 1] = num_ref[4, c + 1 : c + 2]
        num_ref[10, i : i + 1] = num_ref[4, c + 4 : c + 5]
    entry = num_ref[5]
    index = (entry + 64) & 127
    found = num_ref[6]
    for i, least in enumerate((64, 192, 320, 448)):
        found = jnp.where(entry < least, found, lanes_of(num_ref[7 + i], index))
    num_ref[11] = found
    code_ref[0:1] = 64 * slot_of(0, 0, 0) + (iota((1, 128), 1) & 63)
    code_ref[1:2] = coded(1, 0, 0)
    code_ref[2:3] = coded(-1, 0, 0)
    code_ref[3:4] = num_ref[4, 1:2]
    code_ref[4:5] = num_ref[4, 4:5]
    code_ref[5:7] = num_ref[11, 0:2]
    code_ref[7:8] = jnp.zeros((1, 128), I32)
    code = code_ref[...]
    atom = code & 63
    owner = code >> 6
    spots = [jnp.zeros((8, 128), F32)] * 3
    for a, b, c in OFFSETS:
        e = source(a, b, c)
        row_xy = across(recv_ref[e, :, 128:256], 8)
        row_z = recv_ref[e, :, 256:320]
        row_z = across(jnp.concatenate([row_z, row_z], axis=1), 8)
        here = owner == slot_of(a, b, c)
        got = (lanes_of(row_xy, atom), lanes_of(row_xy, atom + 64), lanes_of(row_z, atom))
        spots = [jnp.where(here, g - float(o), s) for g, o, s in zip(got, (a, b, c), spots)]
    for i in range(3):
        ext_ref[i] = spots[i]


def evaluate(
    recv_ref, nb_ref, w2_ref, w2t_ref, w3_ref, w3t_ref, cols_ref, ecols_ref,
    f1_ref, f1t_ref, f2_ref, f2t_ref, f3_ref, f3t_ref,
    out_ref,
    num_ref, ext_ref, code_ref, idx_ref, off_ref, inv_ref, env_ref, hi_ref, lo_ref,
    s1_ref, s2_ref, s3_ref, h3_ref, mom_ref, nat_ref, axis_ref, feat_ref, dfeat_ref,
    dnat_ref, denv_ref, dinv_ref, grad_ref, acc_ref,
):
    count = recv_ref.shape[0]
    me = lax.axis_index("space")
    resolve(me, count, recv_ref, num_ref, ext_ref, code_ref)

    idx_ref[:, 0:64] = nb_ref[0:ROWS, :]
    idx_ref[:, 64:128] = nb_ref[ROWS:K, :]
    for q in range(ROWS // 8):
        at = slice(8 * q, 8 * q + 8)
        ids = idx_ref[at]
        present = jnp.where(ids >= 0, 1.0, 0.0)
        row, lane = (ids + 64) >> 7, (ids + 64) & 127
        spots = [jnp.zeros((8, 128), F32)] * 3
        code = jnp.zeros((8, 128), I32)
        for k in range(7):
            here = row == k
            spots = [
                jnp.where(here, lanes_of(across(ext_ref[i, k : k + 1], 8), lane), s)
                for i, s in enumerate(spots)
            ]
            code = jnp.where(here, lanes_of(across(code_ref[k : k + 1], 8), lane), code)
        offs = [s - ext_ref[i, 0:1] for i, s in enumerate(spots)]
        inverse = lax.rsqrt(offs[0] * offs[0] + offs[1] * offs[1] + offs[2] * offs[2] + SOFTEN)
        inv_ref[at] = inverse
        env_ref[0, at] = inverse * present
        for i in range(3):
            off_ref[i, at] = offs[i]
            env_ref[i + 1, at] = (inverse * inverse) * offs[i] * present
        hi_ref[at] = jnp.where(ids >= 0, code >> 7, -1)
        lo_ref[at] = code & 127

    mom_ref[...] = jnp.zeros_like(mom_ref)
    scale = jnp.broadcast_to(ecols_ref[0:32, 0:1], (32, 128))
    shift = jnp.broadcast_to(ecols_ref[0:32, 1:2], (32, 128))
    constant = (iota((32, 128), 0) == 25) | (iota((32, 128), 0) == 26)
    shift = jnp.where(constant, 40.0, shift)

    def forward(q, carry):
        base = pl.multiple_of(q * 8, 8)
        firsts = []
        for r in range(8):
            t = jnp.tanh(scale * inv_ref[pl.ds(base + r, 1), :] + shift)
            s1_ref[base + r] = (1.0 - t * t).astype(BF16)
            firsts.append(t.astype(BF16))
        h1 = jnp.concatenate(firsts, axis=1)
        t2 = jnp.tanh(dot(w2_ref[...], h1))
        h2 = (jnp.concatenate([h1, h1], axis=0).astype(F32) + t2).astype(BF16)
        s2 = (1.0 - t2 * t2).astype(BF16)
        t3 = jnp.tanh(dot(w3_ref[...], h2))
        h3 = (jnp.concatenate([h2, h2], axis=0).astype(F32) + t3).astype(BF16)
        s3 = (1.0 - t3 * t3).astype(BF16)
        for r in range(8):
            part = slice(128 * r, 128 * r + 128)
            s2_ref[base + r] = s2[:, part]
            s3_ref[base + r] = s3[:, part]
            h3_ref[base + r] = h3[:, part]
        env = [[env_ref[c, pl.ds(base + r, 1), :] for r in range(8)] for c in range(4)]
        for n in range(8):
            rows = slice(16 * n, 16 * n + 16)
            tiles = [h3[rows, 128 * r : 128 * r + 128].astype(F32) for r in range(8)]
            for c in range(4):
                total = tiles[0] * env[c][0]
                for r in range(1, 8):
                    total = total + tiles[r] * env[c][r]
                mom_ref[c, rows] = mom_ref[c, rows] + total.astype(F32)
        return carry

    lax.fori_loop(0, ROWS // 8, forward, 0, unroll=True)

    low = iota((1, 128), 1) < 64
    nat_ref[:, 96:112, :] = jnp.zeros((4, 16, 128), F32)
    for c in range(4):
        m = mom_ref[c]
        m = (m + half_turn(m)) * (1.0 / K)
        for q in range(4):
            nat_ref[c, 25 * q : 25 * q + 25] = m[32 * q : 32 * q + 25]
        axis_ref[c] = jnp.where(low, m[0:8], m[8:16])
    for blk in range(7):
        mine = [nat_ref[c, 16 * blk : 16 * blk + 16] for c in range(4)]
        for p in range(8):
            total = mine[0] * axis_ref[0, p : p + 1]
            for c in range(1, 4):
                total = total + mine[c] * axis_ref[c, p : p + 1]
            feat_ref[128 * blk + 16 * p : 128 * blk + 16 * p + 16] = total.astype(BF16)

    both = dot(f1_ref[...], feat_ref[...])
    pre = jnp.where(low, both[0:240], both[240:480])
    t1 = jnp.tanh(pre + half_turn(pre) + cols_ref[0:240, 4:5])
    g1 = t1.astype(BF16)
    t2 = jnp.tanh(dot(f2_ref[0], g1) + cols_ref[0:240, 5:6])
    g2 = (g1.astype(F32) + t2).astype(BF16)
    t3 = jnp.tanh(dot(f3_ref[0], g2) + cols_ref[0:240, 6:7])
    d3 = jnp.broadcast_to(cols_ref[0:240, 7:8], (240, 128))
    back = dot(f3t_ref[...], (d3 * (1.0 - t3 * t3)).astype(BF16)).astype(BF16).astype(F32)
    d2 = (back + d3).astype(BF16).astype(F32)
    back = dot(f2t_ref[...], (d2 * (1.0 - t2 * t2)).astype(BF16)).astype(BF16).astype(F32)
    d1 = (back + d2).astype(BF16).astype(F32)
    d1 = d1 * (1.0 - t1 * t1)
    none = jnp.zeros((16, 128), F32)
    split = jnp.concatenate([jnp.where(low, d1, 0.0), none, jnp.where(low, 0.0, d1), none], axis=0)
    dfeat_ref[...] = dot(f1t_ref[...], split.astype(BF16)).astype(BF16).astype(F32)

    mom_ref[...] = jnp.zeros_like(mom_ref)
    for c in range(4):
        sums = [jnp.zeros((16, 128), F32)] * 8
        for blk in range(7):
            mine = nat_ref[c, 16 * blk : 16 * blk + 16]
            total = jnp.zeros((16, 128), F32)
            for p in range(8):
                d = dfeat_ref[128 * blk + 16 * p : 128 * blk + 16 * p + 16]
                total = total + d * axis_ref[c, p : p + 1]
                sums[p] = sums[p] + d * mine
            dnat_ref[c, 16 * blk : 16 * blk + 16] = total + half_turn(total)
        rows = jnp.concatenate([jnp.sum(s, axis=0, keepdims=True) for s in sums], axis=0)
        turned = half_turn(rows)
        dnat_ref[c, 0:8] = dnat_ref[c, 0:8] + jnp.where(low, rows, turned)
        dnat_ref[c, 8:16] = dnat_ref[c, 8:16] + jnp.where(low, turned, rows)
        for q in range(4):
            mom_ref[c, 32 * q : 32 * q + 25] = dnat_ref[c, 25 * q : 25 * q + 25] * (1.0 / K)

    def backward(q, carry):
        base = pl.multiple_of(q * 4, 4)
        outer, pushed = [], []
        for r in range(4):
            env = [env_ref[c, pl.ds(base + r, 1), :] for c in range(4)]
            parts = [None] * 4
            tiles = []
            for n in range(8):
                rows = slice(16 * n, 16 * n + 16)
                dm = [mom_ref[c, rows] for c in range(4)]
                tiles.append((dm[0] * env[0] + dm[1] * env[1] + dm[2] * env[2] + dm[3] * env[3]).astype(BF16))
                h = h3_ref[base + r, rows].astype(F32)
                parts = [dm[c] * h if s is None else s + dm[c] * h for c, s in enumerate(parts)]
            for c in range(4):
                denv_ref[c, pl.ds(base + r, 1), :] = jnp.sum(parts[c], axis=0, keepdims=True)
            d = jnp.concatenate(tiles, axis=0)
            outer.append(d)
            pushed.append(d * s3_ref[base + r])
        d3 = jnp.concatenate(outer, axis=1)
        back = dot(w3t_ref[...], jnp.concatenate(pushed, axis=1)).astype(BF16)
        d2 = back + d3[0:64] + d3[64:128]
        s2 = jnp.concatenate([s2_ref[base + r] for r in range(4)], axis=1)
        back = dot(w2t_ref[...], d2 * s2).astype(BF16)
        d1 = (back + d2[0:32] + d2[32:64]).astype(F32)
        for r in range(4):
            d = d1[:, 128 * r : 128 * r + 128] * s1_ref[base + r].astype(F32) * scale
            dinv_ref[pl.ds(base + r, 1), :] = jnp.sum(d, axis=0, keepdims=True)
        return carry

    lax.fori_loop(0, ROWS // 4, backward, 0, unroll=True)

    centre = [jnp.zeros((8, 128), F32)] * 3
    for q in range(ROWS // 8):
        at = slice(8 * q, 8 * q + 8)
        inverse = inv_ref[at]
        present = jnp.where(idx_ref[at] >= 0, 1.0, 0.0)
        offs = [off_ref[i, at] for i in range(3)]
        denv = [denv_ref[c, at] * present for c in range(4)]
        along = denv[1] * offs[0] + denv[2] * offs[1] + denv[3] * offs[2]
        square = inverse * inverse
        slope = (dinv_ref[at] + denv[0] + 2.0 * inverse * along) * (square * inverse) * -1.0
        for i in range(3):
            g = denv[i + 1] * square + slope * offs[i]
            grad_ref[i, at] = g
            centre[i] = centre[i] + g

    acc_ref[...] = jnp.zeros_like(acc_ref)
    which = iota((8, 128), 0)
    lead, next_up, rest = which % 3 == 0, which % 3 == 1, which >= 6
    spot = iota((16, 128), 0).astype(F32).astype(BF16)

    def scatter(q, carry):
        base = pl.multiple_of(q * 8, 8)
        left, right = [], []
        for r in range(8):
            at = pl.ds(base + r, 1)
            gx, gy, gz = (across(grad_ref[i, at, :], 8) for i in range(3))
            ox, oy, oz = (across(off_ref[i, at, :], 8) for i in range(3))
            g_even = jnp.where(lead, gx, jnp.where(next_up, gz, gy))
            o_even = jnp.where((which < 2) | rest, 1.0, jnp.where(which == 2, ox, jnp.where(which < 5, oy, oz)))
            g_odd = jnp.where(lead, gy, jnp.where(next_up, gx, gz))
            o_odd = jnp.where((which < 1) | rest, 1.0, jnp.where(which < 3, ox, jnp.where(which < 4, oy, oz)))
            halves = (-g_even * o_even, -g_odd * o_odd)
            term = jnp.concatenate([jnp.where(rest, t - t.astype(BF16).astype(F32), t) for t in halves], axis=0)
            term = term.astype(BF16)
            high = across(hi_ref[at, :], 16).astype(F32).astype(BF16)
            place = across(lo_ref[at, :], 16).astype(F32).astype(BF16)
            zero, one = jnp.zeros((16, 128), BF16), jnp.ones((16, 128), BF16)
            left.append(jnp.concatenate([jnp.where(high == float(h), term, zero) for h in range(14)], axis=0))
            right.append(
                jnp.concatenate([jnp.where(spot + float(16 * n) == place, one, zero) for n in range(8)], axis=0)
            )
        acc_ref[...] = acc_ref[...] + dot_last(jnp.concatenate(left, axis=1), jnp.concatenate(right, axis=1))
        return carry

    lax.fori_loop(0, ROWS // 8, scatter, 0, unroll=True)

    rows = [jnp.sum(s, axis=0, keepdims=True) for s in centre]
    rows = [s + half_turn(s) for s in rows]
    own = jnp.concatenate(
        [jnp.where(low, rows[0], rows[1]), jnp.where(low, rows[2], 0.0), jnp.zeros((6, 128), F32)], axis=0
    )
    mine = me & (RUN - 1)
    for a, b, c in OFFSETS:
        h, odd = divmod(slot_of(a, b, c), 2)
        even_terms = acc_ref[16 * h : 16 * h + 8]
        odd_terms = acc_ref[16 * h + 8 : 16 * h + 16]
        even_terms = even_terms + jnp.where(which < 2, pltpu.roll(even_terms, 2, axis=0), 0.0)
        odd_terms = odd_terms + jnp.where(which < 1, pltpu.roll(odd_terms, 2, axis=0), 0.0)
        if odd:
            tile = jnp.where(low, half_turn(even_terms), odd_terms)
        else:
            tile = jnp.where(low, even_terms, half_turn(odd_terms))
        if (a, b, c) == (0, 0, 0):
            tile = tile + own
        place = 6 * place_of(a, b, c)
        out_ref[(mine - (4 * b + c)) & (RUN - 1), place : place + 6, :] = tile[0:6]


def regroup(recv_ref, out_ref, sum_ref):
    me = lax.axis_index("space")
    mine, run = me & (RUN - 1), me // RUN
    runs = out_ref.shape[0] // 4
    sum_ref[...] = jnp.zeros_like(sum_ref)
    for a, b, c in OFFSETS:
        moved = mine + 4 * b + c
        away = pl.multiple_of(8 * (SPAN - 2 * a - (moved >> 3)), 8)
        place = 6 * place_of(a, b, c)
        sum_ref[pl.ds(away, 6), :] = sum_ref[pl.ds(away, 6), :] + recv_ref[moved & (RUN - 1), place : place + 6, :]
    parts = [sum_ref[pl.ds(k, 8, stride=8), :] for k in range(6)]
    lane = iota((8, 128), 1) // 16
    for quarter in range(4):
        tiles = [jnp.zeros((8, 128), F32)] * 2
        for side in range(2):
            for k in range(6):
                tile, group = divmod(6 * side + k, 8)
                turn = (16 * (group - quarter) - 64 * side) % 128
                piece = parts[k] if turn == 0 else pltpu.roll(parts[k], turn, axis=1)
                tiles[tile] = jnp.where(lane == group, piece, tiles[tile])
        for o in range(2 * SPAN + 1):
            target = quarter * runs + ((run + o - SPAN) & (runs - 1))
            out_ref[target, :, 0:128] = tiles[0][o : o + 1]
            out_ref[target, :, 128:192] = tiles[1][o : o + 1, 0:64]


def finish(recv_ref, mean_ref, force_ref, virial_ref):
    run = lax.axis_index("space") // RUN
    runs = recv_ref.shape[0] // 4
    totals = []
    for m in range(4):
        total = recv_ref[m * runs + run]
        for o in range(-SPAN, SPAN + 1):
            if o != 0:
                total = total + recv_ref[m * runs + ((run - o) & (runs - 1))]
        totals.append(total)
    mean = (totals[0] + totals[1] + totals[2] + totals[3]) * 0.25
    spread = jnp.zeros_like(mean)
    for total in totals:
        spread = spread + (total - mean) * (total - mean)
    spread = spread * 0.25

    def component(x, k):
        at = 16 * (6 * (k % 2) + k // 2)
        return x[:, at : at + 16]

    for k in range(3):
        mean_ref[k, 0] = component(mean, k)
    force = component(spread, 0)
    for k in range(1, 3):
        force = force + component(spread, k)
    force_ref[0] = force
    virial = component(spread, 3)
    for k in range(4, 12):
        virial = virial + component(spread, k)
    virial_ref[0] = virial


def call(body, out_shape, scratch=(), limit=16 << 20, **specs):
    return pl.pallas_call(
        body,
        out_shape=out_shape,
        scratch_shapes=list(scratch),
        compiler_params=pltpu.CompilerParams(vmem_limit_bytes=limit),
        **specs,
    )


def shaped(shape, dtype=F32):
    return jax.ShapeDtypeStruct(shape, dtype)


def local(
    positions, send_lists, neighbours,
    emb_scale, emb_shift, emb_middle, emb_mid_bias, emb_outer, emb_out_bias,
    fit_first, fit_first_bias, fit_second, fit_second_bias, fit_third, fit_third_bias, fit_readout,
):
    count = lax.axis_size("space")
    models = lax.axis_size("mp")
    runs = count // RUN
    packed = call(
        outgoing,
        shaped((count, 1, 320)),
        [
            pltpu.VMEM((6, 1, 128), I32),
            pltpu.VMEM(positions.shape, F32),
            pltpu.SemaphoreType.DMA((2,)),
        ],
        63 << 20,
        in_specs=[pl.BlockSpec(memory_space=pl.ANY)] * 2,
    )(jnp.transpose(send_lists, (1, 0, 2)), positions)
    arrived = lax.all_to_all(packed, "space", 0, 0)
    w2, w2t, w3, w3t, cols, ecols, f1, f1t, f2t, f3t = call(
        weights,
        (
            shaped((64, 32), BF16), shaped((32, 64), BF16), shaped((128, 64), BF16), shaped((64, 128), BF16),
            shaped((256, 128)), shaped((128, 128)), shaped((480, 896), BF16), shaped((896, 512), BF16),
            shaped((240, 240), BF16), shaped((240, 240), BF16),
        ),
        [pltpu.VMEM((128, 256), F32)],
    )(
        emb_scale, emb_shift, emb_middle, emb_mid_bias, emb_outer, emb_out_bias,
        fit_first, fit_first_bias, fit_second, fit_second_bias, fit_third, fit_third_bias, fit_readout,
    )
    pair = (ROWS, 128)
    terms = call(
        evaluate,
        shaped((RUN, 36, 128)),
        [
            pltpu.VMEM((12, 8, 128), I32), pltpu.VMEM((3, 8, 128), F32), pltpu.VMEM((8, 128), I32),
            pltpu.VMEM(pair, I32), pltpu.VMEM((3, *pair), F32), pltpu.VMEM(pair, F32), pltpu.VMEM((4, *pair), F32),
            pltpu.VMEM(pair, I32), pltpu.VMEM(pair, I32),
            pltpu.VMEM((ROWS, 32, 128), BF16), pltpu.VMEM((ROWS, 64, 128), BF16),
            pltpu.VMEM((ROWS, 128, 128), BF16), pltpu.VMEM((ROWS, 128, 128), BF16),
            pltpu.VMEM((4, 128, 128), F32), pltpu.VMEM((4, 112, 128), F32), pltpu.VMEM((4, 8, 128), F32),
            pltpu.VMEM((896, 128), BF16), pltpu.VMEM((896, 128), F32),
            pltpu.VMEM((4, 112, 128), F32),
            pltpu.VMEM((4, *pair), F32), pltpu.VMEM(pair, F32), pltpu.VMEM((3, *pair), F32),
            pltpu.VMEM((224, 128), F32),
        ],
        32 << 20,
    )(arrived, neighbours, w2, w2t, w3, w3t, cols, ecols, f1, f1t, fit_second, f2t, fit_third, f3t)
    near = [[RUN * u + v for v in range(RUN)] for u in range(runs)]
    terms = lax.all_to_all(terms, "space", 0, 0, axis_index_groups=near)
    terms = call(regroup, shaped((models * runs, 1, 192)), [pltpu.VMEM((64, 128), F32)])(terms)
    far = [[m * count + RUN * u + v for m in range(models) for u in range(runs)] for v in range(RUN)]
    terms = lax.all_to_all(terms, ("mp", "space"), 0, 0, axis_index_groups=far)
    quarter = positions.shape[1] // models
    return call(
        finish, (shaped((3, 1, 1, quarter)), shaped((1, 1, quarter)), shaped((1, 1, quarter)))
    )(terms)


def solution(mesh):
    params = [P("mp", None)] * 2 + [P("mp", None, None), P("mp", None)] * 5 + [P("mp", None)]
    return jax.shard_map(
        local,
        mesh=mesh,
        in_specs=(P(None, "space"), P("space", None, None), P(None, "space"), *params),
        out_specs=(P(None, "space", "mp", None), P("space", "mp", None), P("space", "mp", None)),
        check_vma=False,
    )
```

```python
import jax
import jax.numpy as jnp
from jax import lax
from jax.experimental import pallas as pl
from jax.experimental.pallas import tpu as pltpu
from jax.sharding import PartitionSpec as P

F32, BF16, I32 = jnp.float32, jnp.bfloat16, jnp.int32
K = 96
ROWS = K // 2
SOFTEN = 0.04
RUN = 8
SPAN = 3
OFFSETS = tuple((a, b, c) for a in (-1, 0, 1) for b in (-1, 0, 1) for c in (-1, 0, 1))


def slot_of(a, b, c):
    return (a + 1) * 9 + (b + 1) * 3 + (c + 1)


def step_of(a, b, c):
    return 16 * a + 4 * b + c


def place_of(a, b, c):
    return (3 if 4 * b + c <= -3 else 0) + a + 1


def iota(shape, dim):
    return lax.broadcasted_iota(I32, shape, dim)


def lanes_of(table, index):
    return jnp.take_along_axis(table, index, axis=1, mode="promise_in_bounds")


def across(row, count):
    return jnp.broadcast_to(row, (count, row.shape[1]))


def half_turn(x):
    return pltpu.roll(x, 64, axis=x.ndim - 1)


def dot(a, b):
    return jnp.dot(a, b, preferred_element_type=F32)


def dot_last(a, b):
    return lax.dot_general(a, b, (((1,), (1,)), ((), ())), preferred_element_type=F32)


def outgoing(lists_hbm, pos_hbm, out_ref, lists_ref, pos_ref, sems):
    fetches = [
        pltpu.make_async_copy(lists_hbm, lists_ref, sems.at[0]),
        pltpu.make_async_copy(pos_hbm, pos_ref, sems.at[1]),
    ]
    for fetch in fetches:
        fetch.start()
    for fetch in fetches:
        fetch.wait()
    count = out_ref.shape[0]
    me = lax.axis_index("space")
    lists = lists_ref[:, 0, :].astype(F32)
    pos = pos_ref[...]
    row_xy = jnp.concatenate([pos[0:1], pos[1:2]], axis=1)
    row_z = pos[2:3]
    for a, b, c in OFFSETS:
        target = lax.rem(me + step_of(a, b, c) + count, count)
        block = next((2 * s + (0 if v > 0 else 1) for s, v in enumerate((a, b, c)) if v), None)
        first = jnp.zeros((1, 128), F32) if block is None else lists[block : block + 1]
        out_ref[target, :, 0:128] = first
        out_ref[target, :, 128:256] = row_xy
        out_ref[target, :, 256:320] = row_z


def grouped(rows, cols, by_row):
    r, c = iota((rows, cols), 0), iota((rows, cols), 1)
    wide, narrow = (r, c) if by_row else (c, r)
    hit = (narrow == (wide // 32) * 25 + wide % 32) & (wide % 32 < 25)
    return hit.astype(F32).astype(BF16)


def eye(n):
    return (iota((n, n), 0) == iota((n, n), 1)).astype(F32).astype(BF16)


def weights(
    scale_ref, shift_ref, mid_ref, mid_b_ref, outer_ref, outer_b_ref,
    one_ref, one_b_ref, two_ref, two_b_ref, three_ref, three_b_ref, read_ref,
    w2_ref, w2t_ref, w3_ref, w3t_ref, cols_ref, ecols_ref, f1_ref, f1t_ref, f2t_ref, f3t_ref,
    stack_ref,
):
    w2 = dot(dot(grouped(64, 50, True), mid_ref[0]).astype(BF16), grouped(25, 32, False)).astype(BF16)
    w3 = dot(dot(grouped(128, 100, True), outer_ref[0]).astype(BF16), grouped(50, 64, False)).astype(BF16)
    w2t_ref[...] = dot_last(eye(32), w2).astype(BF16)
    w3t_ref[...] = dot_last(eye(64), w3).astype(BF16)
    f2t_ref[...] = dot_last(eye(240), two_ref[0]).astype(BF16)
    f3t_ref[...] = dot_last(eye(240), three_ref[0]).astype(BF16)
    stack_ref[...] = jnp.zeros_like(stack_ref)
    small = (scale_ref, shift_ref, mid_b_ref, outer_b_ref, one_b_ref, two_b_ref, three_b_ref, read_ref)
    for i, ref in enumerate(small):
        stack_ref[i : i + 1, 0 : ref.shape[1]] = ref[...].astype(F32)
    turned = jnp.transpose(stack_ref[...], (1, 0))
    cols_ref[...] = turned
    ecols_ref[...] = jnp.zeros_like(ecols_ref)
    for q in range(4):
        ecols_ref[32 * q : 32 * q + 25, :] = turned[25 * q : 25 * q + 25]
    for w, ref, column in ((w2, w2_ref, 2), (w3, w3_ref, 3)):
        bias = jnp.broadcast_to(ecols_ref[0 : w.shape[0], column : column + 1], w.shape)
        whole = bias.astype(BF16).astype(F32)
        lane = iota(w.shape, 1)
        ref[...] = jnp.where(lane == 25, whole, jnp.where(lane == 26, bias - whole, w.astype(F32))).astype(BF16)
    f1t_ref[...] = jnp.zeros_like(f1t_ref)
    for part in range(2):
        r, c = iota((256, 128), 0), iota((256, 128), 1)
        pick = (r == (c % 16) * 16 + c // 16 + 8 * part).astype(F32).astype(BF16)
        r, c = iota((128, 256), 0), iota((128, 256), 1)
        pick_t = (c == (r % 16) * 16 + r // 16 + 8 * part).astype(F32).astype(BF16)
        for blk in range(7):
            wide = min(256, 1600 - 256 * blk)
            piece = one_ref[0, :, 256 * blk : 256 * blk + wide]
            f1_ref[240 * part : 240 * part + 240, 128 * blk : 128 * blk + 128] = dot(
                piece, pick[0:wide]
            ).astype(BF16)
            f1t_ref[128 * blk : 128 * blk + 128, 256 * part : 256 * part + 240] = dot_last(
                pick_t[:, 0:wide], piece
            ).astype(BF16)


def resolve(me, count, recv_ref, num_ref, ext_ref, code_ref):
    def source(a, b, c):
        return lax.rem(me - step_of(a, b, c) + count, count)

    def listed(a, b, c):
        return recv_ref[source(a, b, c), :, 0:128].astype(I32)

    def coded(a, b, c):
        return listed(a, b, c) + 64 * slot_of(a, b, c)

    num_ref[...] = jnp.zeros_like(num_ref)
    pairs = [(b, c) for b in (1, -1) for c in (-1, 0, 1)]
    for i, (b, c) in enumerate(pairs):
        entry = listed(0, b, c)
        num_ref[0, i : i + 1] = entry
        num_ref[1, i : i + 1] = entry + 64 * slot_of(0, b, c)
        num_ref[2, i : i + 1] = coded(1, b, c)
        num_ref[3, i : i + 1] = coded(-1, b, c)
    entry = num_ref[0]
    index = (entry + 64) & 127
    middle = jnp.where(
        entry < 64,
        num_ref[1],
        jnp.where(entry < 192, lanes_of(num_ref[2], index), lanes_of(num_ref[3], index)),
    )
    num_ref[4] = middle
    for i, c in enumerate((1, -1)):
        entry = listed(0, 0, c)
        num_ref[5, i : i + 1] = entry
        num_ref[6, i : i + 1] = entry + 64 * slot_of(0, 0, c)
        num_ref[7, i : i + 1] = coded(1, 0, c)
        num_ref[8, i : i + 1] = coded(-1, 0, c)
        num_ref[9, i : i + 1] = num_ref[4, c + 1 : c + 2]
        num_ref[10, i : i + 1] = num_ref[4, c + 4 : c + 5]
    entry = num_ref[5]
    index = (entry + 64) & 127
    found = num_ref[6]
    for i, least in enumerate((64, 192, 320, 448)):
        found = jnp.where(entry < least, found, lanes_of(num_ref[7 + i], index))
    num_ref[11] = found
    code_ref[0:1] = 64 * slot_of(0, 0, 0) + (iota((1, 128), 1) & 63)
    code_ref[1:2] = coded(1, 0, 0)
    code_ref[2:3] = coded(-1, 0, 0)
    code_ref[3:4] = num_ref[4, 1:2]
    code_ref[4:5] = num_ref[4, 4:5]
    code_ref[5:7] = num_ref[11, 0:2]
    code_ref[7:8] = jnp.zeros((1, 128), I32)
    code = code_ref[...]
    atom = code & 63
    owner = code >> 6
    spots = [jnp.zeros((8, 128), F32)] * 3
    for a, b, c in OFFSETS:
        e = source(a, b, c)
        row_xy = across(recv_ref[e, :, 128:256], 8)
        row_z = recv_ref[e, :, 256:320]
        row_z = across(jnp.concatenate([row_z, row_z], axis=1), 8)
        here = owner == slot_of(a, b, c)
        got = (lanes_of(row_xy, atom), lanes_of(row_xy, atom + 64), lanes_of(row_z, atom))
        spots = [jnp.where(here, g - float(o), s) for g, o, s in zip(got, (a, b, c), spots)]
    for i in range(3):
        ext_ref[i] = spots[i]


def evaluate(
    recv_ref, nb_ref, w2_ref, w2t_ref, w3_ref, w3t_ref, cols_ref, ecols_ref,
    f1_ref, f1t_ref, f2_ref, f2t_ref, f3_ref, f3t_ref,
    out_ref,
    num_ref, ext_ref, code_ref, idx_ref, off_ref, inv_ref, env_ref, hi_ref, lo_ref,
    s1_ref, s2_ref, s3_ref, h3_ref, mom_ref, nat_ref, axis_ref, feat_ref, dfeat_ref,
    dnat_ref, denv_ref, dinv_ref, grad_ref, acc_ref,
):
    count = recv_ref.shape[0]
    me = lax.axis_index("space")
    resolve(me, count, recv_ref, num_ref, ext_ref, code_ref)

    idx_ref[:, 0:64] = nb_ref[0:ROWS, :]
    idx_ref[:, 64:128] = nb_ref[ROWS:K, :]
    for q in range(ROWS // 8):
        at = slice(8 * q, 8 * q + 8)
        ids = idx_ref[at]
        present = jnp.where(ids >= 0, 1.0, 0.0)
        row, lane = (ids + 64) >> 7, (ids + 64) & 127
        spots = [jnp.zeros((8, 128), F32)] * 3
        code = jnp.zeros((8, 128), I32)
        for k in range(7):
            here = row == k
            spots = [
                jnp.where(here, lanes_of(across(ext_ref[i, k : k + 1], 8), lane), s)
                for i, s in enumerate(spots)
            ]
            code = jnp.where(here, lanes_of(across(code_ref[k : k + 1], 8), lane), code)
        offs = [s - ext_ref[i, 0:1] for i, s in enumerate(spots)]
        inverse = lax.rsqrt(offs[0] * offs[0] + offs[1] * offs[1] + offs[2] * offs[2] + SOFTEN)
        inv_ref[at] = inverse
        env_ref[0, at] = inverse * present
        for i in range(3):
            off_ref[i, at] = offs[i]
            env_ref[i + 1, at] = (inverse * inverse) * offs[i] * present
        hi_ref[at] = jnp.where(ids >= 0, code >> 7, -1)
        lo_ref[at] = code & 127

    mom_ref[...] = jnp.zeros_like(mom_ref)
    scale = jnp.broadcast_to(ecols_ref[0:32, 0:1], (32, 128))
    shift = jnp.broadcast_to(ecols_ref[0:32, 1:2], (32, 128))
    constant = (iota((32, 128), 0) == 25) | (iota((32, 128), 0) == 26)
    shift = jnp.where(constant, 40.0, shift)

    def forward(q, carry):
        base = pl.multiple_of(q * 12, 4)
        firsts = []
        for r in range(12):
            t = jnp.tanh(scale * inv_ref[pl.ds(base + r, 1), :] + shift)
            s1_ref[base + r] = (1.0 - t * t).astype(BF16)
            firsts.append(t.astype(BF16))
        h1 = jnp.concatenate(firsts, axis=1)
        t2 = jnp.tanh(dot(w2_ref[...], h1))
        h2 = (jnp.concatenate([h1, h1], axis=0).astype(F32) + t2).astype(BF16)
        s2 = (1.0 - t2 * t2).astype(BF16)
        t3 = jnp.tanh(dot(w3_ref[...], h2))
        h3 = (jnp.concatenate([h2, h2], axis=0).astype(F32) + t3).astype(BF16)
        s3 = (1.0 - t3 * t3).astype(BF16)
        for r in range(12):
            part = slice(128 * r, 128 * r + 128)
            s2_ref[base + r] = s2[:, part]
            s3_ref[base + r] = s3[:, part]
            h3_ref[base + r] = h3[:, part]
        env = [[env_ref[c, pl.ds(base + r, 1), :] for r in range(12)] for c in range(4)]
        for n in range(8):
            rows = slice(16 * n, 16 * n + 16)
            tiles = [h3[rows, 128 * r : 128 * r + 128].astype(F32) for r in range(12)]
            for c in range(4):
                total = tiles[0] * env[c][0]
                for r in range(1, 12):
                    total = total + tiles[r] * env[c][r]
                mom_ref[c, rows] = mom_ref[c, rows] + total.astype(F32)
        return carry

    lax.fori_loop(0, ROWS // 12, forward, 0, unroll=True)

    low = iota((1, 128), 1) < 64
    nat_ref[:, 96:112, :] = jnp.zeros((4, 16, 128), F32)
    for c in range(4):
        m = mom_ref[c]
        m = (m + half_turn(m)) * (1.0 / K)
        for q in range(4):
            nat_ref[c, 25 * q : 25 * q + 25] = m[32 * q : 32 * q + 25]
        axis_ref[c] = jnp.where(low, m[0:8], m[8:16])
    for blk in range(7):
        mine = [nat_ref[c, 16 * blk : 16 * blk + 16] for c in range(4)]
        for p in range(8):
            total = mine[0] * axis_ref[0, p : p + 1]
            for c in range(1, 4):
                total = total + mine[c] * axis_ref[c, p : p + 1]
            feat_ref[128 * blk + 16 * p : 128 * blk + 16 * p + 16] = total.astype(BF16)

    both = dot(f1_ref[...], feat_ref[...])
    pre = jnp.where(low, both[0:240], both[240:480])
    t1 = jnp.tanh(pre + half_turn(pre) + cols_ref[0:240, 4:5])
    g1 = t1.astype(BF16)
    t2 = jnp.tanh(dot(f2_ref[0], g1) + cols_ref[0:240, 5:6])
    g2 = (g1.astype(F32) + t2).astype(BF16)
    t3 = jnp.tanh(dot(f3_ref[0], g2) + cols_ref[0:240, 6:7])
    d3 = jnp.broadcast_to(cols_ref[0:240, 7:8], (240, 128))
    back = dot(f3t_ref[...], (d3 * (1.0 - t3 * t3)).astype(BF16)).astype(BF16).astype(F32)
    d2 = (back + d3).astype(BF16).astype(F32)
    back = dot(f2t_ref[...], (d2 * (1.0 - t2 * t2)).astype(BF16)).astype(BF16).astype(F32)
    d1 = (back + d2).astype(BF16).astype(F32)
    d1 = d1 * (1.0 - t1 * t1)
    none = jnp.zeros((16, 128), F32)
    split = jnp.concatenate([jnp.where(low, d1, 0.0), none, jnp.where(low, 0.0, d1), none], axis=0)
    dfeat_ref[...] = dot(f1t_ref[...], split.astype(BF16)).astype(BF16).astype(F32)

    mom_ref[...] = jnp.zeros_like(mom_ref)
    for c in range(4):
        sums = [jnp.zeros((16, 128), F32)] * 8
        for blk in range(7):
            mine = nat_ref[c, 16 * blk : 16 * blk + 16]
            total = jnp.zeros((16, 128), F32)
            for p in range(8):
                d = dfeat_ref[128 * blk + 16 * p : 128 * blk + 16 * p + 16]
                total = total + d * axis_ref[c, p : p + 1]
                sums[p] = sums[p] + d * mine
            dnat_ref[c, 16 * blk : 16 * blk + 16] = total + half_turn(total)
        rows = jnp.concatenate([jnp.sum(s, axis=0, keepdims=True) for s in sums], axis=0)
        turned = half_turn(rows)
        dnat_ref[c, 0:8] = dnat_ref[c, 0:8] + jnp.where(low, rows, turned)
        dnat_ref[c, 8:16] = dnat_ref[c, 8:16] + jnp.where(low, turned, rows)
        for q in range(4):
            mom_ref[c, 32 * q : 32 * q + 25] = dnat_ref[c, 25 * q : 25 * q + 25] * (1.0 / K)

    def backward(q, carry):
        base = pl.multiple_of(q * 4, 4)
        outer, pushed = [], []
        for r in range(4):
            env = [env_ref[c, pl.ds(base + r, 1), :] for c in range(4)]
            parts = [None] * 4
            tiles = []
            for n in range(8):
                rows = slice(16 * n, 16 * n + 16)
                dm = [mom_ref[c, rows] for c in range(4)]
                tiles.append((dm[0] * env[0] + dm[1] * env[1] + dm[2] * env[2] + dm[3] * env[3]).astype(BF16))
                h = h3_ref[base + r, rows].astype(F32)
                parts = [dm[c] * h if s is None else s + dm[c] * h for c, s in enumerate(parts)]
            for c in range(4):
                denv_ref[c, pl.ds(base + r, 1), :] = jnp.sum(parts[c], axis=0, keepdims=True)
            d = jnp.concatenate(tiles, axis=0)
            outer.append(d)
            pushed.append(d * s3_ref[base + r])
        d3 = jnp.concatenate(outer, axis=1)
        back = dot(w3t_ref[...], jnp.concatenate(pushed, axis=1)).astype(BF16)
        d2 = back + d3[0:64] + d3[64:128]
        s2 = jnp.concatenate([s2_ref[base + r] for r in range(4)], axis=1)
        back = dot(w2t_ref[...], d2 * s2).astype(BF16)
        d1 = (back + d2[0:32] + d2[32:64]).astype(F32)
        for r in range(4):
            d = d1[:, 128 * r : 128 * r + 128] * s1_ref[base + r].astype(F32) * scale
            dinv_ref[pl.ds(base + r, 1), :] = jnp.sum(d, axis=0, keepdims=True)
        return carry

    lax.fori_loop(0, ROWS // 4, backward, 0, unroll=True)

    centre = [jnp.zeros((8, 128), F32)] * 3
    for q in range(ROWS // 8):
        at = slice(8 * q, 8 * q + 8)
        inverse = inv_ref[at]
        present = jnp.where(idx_ref[at] >= 0, 1.0, 0.0)
        offs = [off_ref[i, at] for i in range(3)]
        denv = [denv_ref[c, at] * present for c in range(4)]
        along = denv[1] * offs[0] + denv[2] * offs[1] + denv[3] * offs[2]
        square = inverse * inverse
        slope = (dinv_ref[at] + denv[0] + 2.0 * inverse * along) * (square * inverse) * -1.0
        for i in range(3):
            g = denv[i + 1] * square + slope * offs[i]
            grad_ref[i, at] = g
            centre[i] = centre[i] + g

    acc_ref[...] = jnp.zeros_like(acc_ref)
    which = iota((8, 128), 0)
    lead, next_up, rest = which % 3 == 0, which % 3 == 1, which >= 6
    spot = iota((16, 128), 0).astype(F32).astype(BF16)

    def scatter(q, carry):
        base = pl.multiple_of(q * 8, 8)
        left, right = [], []
        for r in range(8):
            at = pl.ds(base + r, 1)
            gx, gy, gz = (across(grad_ref[i, at, :], 8) for i in range(3))
            ox, oy, oz = (across(off_ref[i, at, :], 8) for i in range(3))
            g_even = jnp.where(lead, gx, jnp.where(next_up, gz, gy))
            o_even = jnp.where((which < 2) | rest, 1.0, jnp.where(which == 2, ox, jnp.where(which < 5, oy, oz)))
            g_odd = jnp.where(lead, gy, jnp.where(next_up, gx, gz))
            o_odd = jnp.where((which < 1) | rest, 1.0, jnp.where(which < 3, ox, jnp.where(which < 4, oy, oz)))
            halves = (-g_even * o_even, -g_odd * o_odd)
            term = jnp.concatenate([jnp.where(rest, t - t.astype(BF16).astype(F32), t) for t in halves], axis=0)
            term = term.astype(BF16)
            high = across(hi_ref[at, :], 16).astype(F32).astype(BF16)
            place = across(lo_ref[at, :], 16).astype(F32).astype(BF16)
            zero, one = jnp.zeros((16, 128), BF16), jnp.ones((16, 128), BF16)
            left.append(jnp.concatenate([jnp.where(high == float(h), term, zero) for h in range(14)], axis=0))
            right.append(
                jnp.concatenate([jnp.where(spot + float(16 * n) == place, one, zero) for n in range(8)], axis=0)
            )
        acc_ref[...] = acc_ref[...] + dot_last(jnp.concatenate(left, axis=1), jnp.concatenate(right, axis=1))
        return carry

    lax.fori_loop(0, ROWS // 8, scatter, 0, unroll=True)

    rows = [jnp.sum(s, axis=0, keepdims=True) for s in centre]
    rows = [s + half_turn(s) for s in rows]
    own = jnp.concatenate(
        [jnp.where(low, rows[0], rows[1]), jnp.where(low, rows[2], 0.0), jnp.zeros((6, 128), F32)], axis=0
    )
    mine = me & (RUN - 1)
    for a, b, c in OFFSETS:
        h, odd = divmod(slot_of(a, b, c), 2)
        even_terms = acc_ref[16 * h : 16 * h + 8]
        odd_terms = acc_ref[16 * h + 8 : 16 * h + 16]
        even_terms = even_terms + jnp.where(which < 2, pltpu.roll(even_terms, 2, axis=0), 0.0)
        odd_terms = odd_terms + jnp.where(which < 1, pltpu.roll(odd_terms, 2, axis=0), 0.0)
        if odd:
            tile = jnp.where(low, half_turn(even_terms), odd_terms)
        else:
            tile = jnp.where(low, even_terms, half_turn(odd_terms))
        if (a, b, c) == (0, 0, 0):
            tile = tile + own
        place = 6 * place_of(a, b, c)
        out_ref[(mine - (4 * b + c)) & (RUN - 1), place : place + 6, :] = tile[0:6]


def regroup(recv_ref, out_ref, sum_ref):
    me = lax.axis_index("space")
    mine, run = me & (RUN - 1), me // RUN
    runs = out_ref.shape[0] // 4
    sum_ref[...] = jnp.zeros_like(sum_ref)
    for a, b, c in OFFSETS:
        moved = mine + 4 * b + c
        away = pl.multiple_of(8 * (SPAN - 2 * a - (moved >> 3)), 8)
        place = 6 * place_of(a, b, c)
        sum_ref[pl.ds(away, 6), :] = sum_ref[pl.ds(away, 6), :] + recv_ref[moved & (RUN - 1), place : place + 6, :]
    parts = [sum_ref[pl.ds(k, 8, stride=8), :] for k in range(6)]
    lane = iota((8, 128), 1) // 16
    for quarter in range(4):
        tiles = [jnp.zeros((8, 128), F32)] * 2
        for side in range(2):
            for k in range(6):
                tile, group = divmod(6 * side + k, 8)
                turn = (16 * (group - quarter) - 64 * side) % 128
                piece = parts[k] if turn == 0 else pltpu.roll(parts[k], turn, axis=1)
                tiles[tile] = jnp.where(lane == group, piece, tiles[tile])
        for o in range(2 * SPAN + 1):
            target = quarter * runs + ((run + o - SPAN) & (runs - 1))
            out_ref[target, :, 0:128] = tiles[0][o : o + 1]
            out_ref[target, :, 128:192] = tiles[1][o : o + 1, 0:64]


def finish(recv_ref, mean_ref, force_ref, virial_ref):
    run = lax.axis_index("space") // RUN
    runs = recv_ref.shape[0] // 4
    totals = []
    for m in range(4):
        total = recv_ref[m * runs + run]
        for o in range(-SPAN, SPAN + 1):
            if o != 0:
                total = total + recv_ref[m * runs + ((run - o) & (runs - 1))]
        totals.append(total)
    mean = (totals[0] + totals[1] + totals[2] + totals[3]) * 0.25
    spread = jnp.zeros_like(mean)
    for total in totals:
        spread = spread + (total - mean) * (total - mean)
    spread = spread * 0.25

    def component(x, k):
        at = 16 * (6 * (k % 2) + k // 2)
        return x[:, at : at + 16]

    for k in range(3):
        mean_ref[k, 0] = component(mean, k)
    force = component(spread, 0)
    for k in range(1, 3):
        force = force + component(spread, k)
    force_ref[0] = force
    virial = component(spread, 3)
    for k in range(4, 12):
        virial = virial + component(spread, k)
    virial_ref[0] = virial


def call(body, out_shape, scratch=(), limit=16 << 20, **specs):
    return pl.pallas_call(
        body,
        out_shape=out_shape,
        scratch_shapes=list(scratch),
        compiler_params=pltpu.CompilerParams(vmem_limit_bytes=limit),
        **specs,
    )


def shaped(shape, dtype=F32):
    return jax.ShapeDtypeStruct(shape, dtype)


def local(
    positions, send_lists, neighbours,
    emb_scale, emb_shift, emb_middle, emb_mid_bias, emb_outer, emb_out_bias,
    fit_first, fit_first_bias, fit_second, fit_second_bias, fit_third, fit_third_bias, fit_readout,
):
    count = lax.axis_size("space")
    models = lax.axis_size("mp")
    runs = count // RUN
    packed = call(
        outgoing,
        shaped((count, 1, 320)),
        [
            pltpu.VMEM((6, 1, 128), I32),
            pltpu.VMEM(positions.shape, F32),
            pltpu.SemaphoreType.DMA((2,)),
        ],
        63 << 20,
        in_specs=[pl.BlockSpec(memory_space=pl.ANY)] * 2,
    )(jnp.transpose(send_lists, (1, 0, 2)), positions)
    arrived = lax.all_to_all(packed, "space", 0, 0)
    w2, w2t, w3, w3t, cols, ecols, f1, f1t, f2t, f3t = call(
        weights,
        (
            shaped((64, 32), BF16), shaped((32, 64), BF16), shaped((128, 64), BF16), shaped((64, 128), BF16),
            shaped((256, 128)), shaped((128, 128)), shaped((480, 896), BF16), shaped((896, 512), BF16),
            shaped((240, 240), BF16), shaped((240, 240), BF16),
        ),
        [pltpu.VMEM((128, 256), F32)],
    )(
        emb_scale, emb_shift, emb_middle, emb_mid_bias, emb_outer, emb_out_bias,
        fit_first, fit_first_bias, fit_second, fit_second_bias, fit_third, fit_third_bias, fit_readout,
    )
    pair = (ROWS, 128)
    terms = call(
        evaluate,
        shaped((RUN, 36, 128)),
        [
            pltpu.VMEM((12, 8, 128), I32), pltpu.VMEM((3, 8, 128), F32), pltpu.VMEM((8, 128), I32),
            pltpu.VMEM(pair, I32), pltpu.VMEM((3, *pair), F32), pltpu.VMEM(pair, F32), pltpu.VMEM((4, *pair), F32),
            pltpu.VMEM(pair, I32), pltpu.VMEM(pair, I32),
            pltpu.VMEM((ROWS, 32, 128), BF16), pltpu.VMEM((ROWS, 64, 128), BF16),
            pltpu.VMEM((ROWS, 128, 128), BF16), pltpu.VMEM((ROWS, 128, 128), BF16),
            pltpu.VMEM((4, 128, 128), F32), pltpu.VMEM((4, 112, 128), F32), pltpu.VMEM((4, 8, 128), F32),
            pltpu.VMEM((896, 128), BF16), pltpu.VMEM((896, 128), F32),
            pltpu.VMEM((4, 112, 128), F32),
            pltpu.VMEM((4, *pair), F32), pltpu.VMEM(pair, F32), pltpu.VMEM((3, *pair), F32),
            pltpu.VMEM((224, 128), F32),
        ],
        32 << 20,
    )(arrived, neighbours, w2, w2t, w3, w3t, cols, ecols, f1, f1t, fit_second, f2t, fit_third, f3t)
    near = [[RUN * u + v for v in range(RUN)] for u in range(runs)]
    terms = lax.all_to_all(terms, "space", 0, 0, axis_index_groups=near)
    terms = call(regroup, shaped((models * runs, 1, 192)), [pltpu.VMEM((64, 128), F32)])(terms)
    far = [[m * count + RUN * u + v for m in range(models) for u in range(runs)] for v in range(RUN)]
    terms = lax.all_to_all(terms, ("mp", "space"), 0, 0, axis_index_groups=far)
    quarter = positions.shape[1] // models
    return call(
        finish, (shaped((3, 1, 1, quarter)), shaped((1, 1, quarter)), shaped((1, 1, quarter)))
    )(terms)


def solution(mesh):
    params = [P("mp", None)] * 2 + [P("mp", None, None), P("mp", None)] * 5 + [P("mp", None)]
    return jax.shard_map(
        local,
        mesh=mesh,
        in_specs=(P(None, "space"), P("space", None, None), P(None, "space"), *params),
        out_specs=(P(None, "space", "mp", None), P("space", "mp", None), P("space", "mp", None)),
        check_vma=False,
    )
```
